32 devices in a mesh: groups: 2 (over y), sect: 4 (over x, core), hid: 4 (over z).
Axes of the slice: x: 2, y: 2, z: 4, core: 2. Of those that a mesh axis runs over, the one named last changes fastest.
Arguments:
- resid: bfloat16 [1024, 4096], P(('groups', 'sect'), 'hid'), parts along dimension 0, may hold values from -64 to 64
- moe_gain: bfloat16 [4096], replicated, may hold values from 0.25 to 1.75
- routes: int32 [1024, 2], P(('groups', 'sect')), parts along dimension 0, may hold values from 0 to 3, all different within a row; in each aligned block of 128 rows (0 to 127, 128 to 255, ...) at most 128 rows name the same one
- gate_q: int32 [1024, 2], P(('groups', 'sect')), parts along dimension 0, may hold values from 16 to 255
- doc_lengths: int32 [8, 4], P(('groups', 'sect')), parts along dimension 0, may hold values from 1 to 64, 128 in all within a row
- w_gate: bfloat16 [4, 4096, 4096], P('sect', None, 'hid'), may hold values from -0.09375 to 0.09375
- w_up: bfloat16 [4, 4096, 4096], P('sect', None, 'hid'), may hold values from -0.09375 to 0.09375
- w_down: bfloat16 [4, 4096, 4096], P('sect', 'hid'), may hold values from -0.09375 to 0.09375
- attn_gain: bfloat16 [4096], replicated, may hold values from 0.25 to 1.75
- w_q: bfloat16 [4096, 4096], P('sect', 'hid')
- w_k: bfloat16 [4096, 1024], P('sect', 'hid')
- w_v: bfloat16 [4096, 1024], P('sect', 'hid'), may hold values from -0.09375 to 0.09375
Outputs:
- new_resid: bfloat16 [1024, 4096], P(('groups', 'sect'), 'hid'), parts along dimension 0
- context: bfloat16 [1024, 4096], P(('groups', 'sect'), 'hid'), parts along dimension 0
The draws below stay inside these ranges and needn't reach their ends.
There are 2 independent parts, one for each index of `groups`. The reference program is written for one: setup_inputs(seed, part) draws one part's arguments, and reference() takes and returns one part's arrays. A program takes and returns all parts, laid end to end along the dimension named above; an argument that names none is the same for every part. Nothing has to cross between parts.
Inputs may be any that keep to these rules, and one draw needn't show every extreme that they name: `routes`: within the rows of one index of sect (aligned blocks of 128 rows) no expert is named by more than 128 rows. `doc_lengths`: each row sums to 128.
All inputs are finite; a program needn't handle non-finite values.
Results may differ from the reference program's by a relative error of at most 0.012.
The reference program's roundings to bfloat16 on the way count: a program that leaves them out, or rounds other values in their place, can miss the bound.
Values may be sent and summed in bfloat16 or wider, within the bound.
No kernel may reach another device: no remote copies, remote signals or barrier semaphores. Data moves between devices by JAX's collectives and lax.ppermute only.
A program may use at most 128 MiB of HBM per device.

```python
import math
import jax
import jax.numpy as jnp
import numpy as np
from jax import lax

D = 4096
H = 32
KVH = 8
HD = 128
FF = 4096
TOK_DEV = 128
NDOC = 4
EXPERTS = 4
CAP = 128
TOKENS = 512
N_SECT = 4


def draw_resid(key, part):
    first, second, third = jax.random.split(key, 3)
    col_scale = jnp.exp(jax.random.uniform(second, (D,), jnp.float32, math.log(0.3), math.log(3.0)))
    row_scale = jnp.exp(jax.random.uniform(third, (TOKENS, 1), jnp.float32, math.log(0.3), math.log(3.0)))
    base = jnp.clip(jax.random.normal(first, (TOKENS, D), jnp.float32), -4.0, 4.0)
    return (base * row_scale * col_scale[None, :]).astype(jnp.bfloat16)


def query_weights(key):
    base = jnp.clip(jax.random.normal(jax.random.fold_in(key, 11), (D, H * HD), jnp.float32), -4.0, 4.0)
    return base / math.sqrt(D)


def draw_w_q(key, part):
    return query_weights(key).astype(jnp.bfloat16)


def draw_w_k(key, part):
    own = jnp.clip(jax.random.normal(jax.random.fold_in(key, 12), (D, KVH * HD), jnp.float32), -4.0, 4.0) / math.sqrt(D)
    result = own
    return result.astype(jnp.bfloat16)


def touch_ends(array, rng, least, top_value):
    spot = [jax.random.randint(jax.random.fold_in(rng, axis), (), 0, length) for axis, length in enumerate(array.shape)]
    widest = array.shape.index(max(array.shape))
    beside = spot[:widest] + [(spot[widest] + 1) % array.shape[widest]] + spot[widest + 1:]
    return array.at[tuple(spot)].set(least).at[tuple(beside)].set(top_value)


def shard_levels(rng, extent, shards, smallest, largest):
    level = 1.0
    for axis_at, blocks in shards:
        draws = jax.random.uniform(jax.random.fold_in(jax.random.fold_in(rng, 6), axis_at), (blocks,), jnp.float32, smallest / len(shards), largest / len(shards))
        level = level * jnp.repeat(jnp.exp(draws), extent[axis_at] // blocks).reshape((-1,) + (1,) * (len(extent) - 1 - axis_at))
    return level


def split_up(count, total, most, skew):
    loads = [(1 << 20) // math.isqrt(standing ** skew) + 1 for standing in range(2, count + 1)]
    surplus, counts = total - most - (count - 1), [1] * (count - 1)
    while surplus > 0:
        candidates = [i for i in range(count - 1) if counts[i] < most]
        pool, remaining = sum([loads[i] for i in candidates]), surplus
        for i in candidates:
            addition = min(most - counts[i], max(1, remaining * loads[i] // pool), surplus)
            counts[i] = counts[i] + addition
            surplus = surplus - addition
    return np.array([most] + counts)


def ragged_sizes(stream_key, count, total, bound, skew):
    if count == 2:
        one = jax.random.randint(stream_key, (), max(1, total - bound), min(bound, total - 1) + 1)
        return jnp.stack([one, total - one])
    tallies = jnp.asarray(split_up(count, total, bound, skew), jnp.int32)
    couples = (count - 1) // 2
    source_of, receiver = tallies[1:1 + 2 * couples:2], tallies[2:2 + 2 * couples:2]
    margin = jnp.minimum(source_of - 1, bound - receiver)
    passed = jax.random.randint(jax.random.fold_in(stream_key, 1), (couples,), 0, 1 << 20) % (margin + 1)
    tallies = tallies.at[1:1 + 2 * couples:2].set(source_of - passed).at[2:2 + 2 * couples:2].set(receiver + passed)
    return tallies[jax.random.permutation(jax.random.fold_in(stream_key, 2), count)]


def assign_block(stream_key, own, number, rows, amount, top, limit, skew):
    ranking = jax.random.permutation(stream_key, amount)
    crowded, usual = shares(amount, rows * top, limit, skew, True), shares(amount, rows * top, limit, skew, False)
    places = jnp.arange(amount)

    def named(tallies, rotation):
        used = int((tallies > 0).sum())
        fixed = max(1, used // 4)
        shifted = fixed + (places - fixed + rotation * (used - fixed)) % max(1, amount - fixed)
        return jnp.zeros((amount,), jnp.int32).at[ranking[jnp.where(places < fixed, places, shifted)]].set(jnp.asarray(tallies, jnp.int32))

    tallies = jnp.where(number % 4 == 0, named(crowded, number // 4), named(usual, number - number // 4 - 1))
    mixed = jax.random.permutation(jax.random.fold_in(own, 3), amount)
    source_of, sink = mixed[0:amount // 2 * 2:2], mixed[1:amount // 2 * 2:2]
    slack = jnp.minimum(tallies[source_of] - 1, limit - tallies[sink]) // 2
    slack = jnp.where((source_of == ranking[0]) | (sink == ranking[0]) | (tallies[sink] == 0), 0, jnp.maximum(slack, 0))
    shifted = jax.random.randint(jax.random.fold_in(own, 4), (amount // 2,), 0, 1 << 20) % (slack + 1)
    tallies = tallies.at[source_of].add(-shifted).at[sink].add(shifted)
    labels = jnp.searchsorted(jnp.cumsum(tallies), jnp.arange(rows * top), side="right").astype(jnp.int32)
    grid = labels.reshape(top, rows).T
    grid = grid[jax.random.permutation(jax.random.fold_in(own, 1), rows)]
    rotation = jax.random.randint(jax.random.fold_in(own, 2), (rows, 1), 0, top)
    return jnp.take_along_axis(grid, (jnp.arange(top)[None, :] + rotation) % top, axis=1)


def shares(count, total, reach, lean, full):
    weights = [(1 << 20) // math.isqrt(rank ** lean) + 1 for rank in range(1, count + 1)]
    largest = reach if full else min(reach, max(-(-total // count), total * weights[0] // sum(weights)))
    least = 1 if total - largest >= count - 1 else 0
    counts, rest = [largest] + [least] * (count - 1), total - largest - least * (count - 1)
    while rest > 0:
        free = [i for i in range(1, count) if counts[i] < largest] or [i for i in range(1, count) if counts[i] < reach]
        mass, left = sum([weights[i] for i in free]), rest
        for i in free:
            addition = min(reach - counts[i], max(1, left * weights[i] // mass), rest)
            counts[i] = counts[i] + addition
            rest = rest - addition
    return np.array(counts)


def scatter_about(key, shape, scale, bound, pieces=(), kind=jnp.bfloat16):
    drawn = scale * jax.random.normal(key, shape, jnp.float32)
    if pieces:
        drawn = drawn * shard_levels(key, shape, pieces, -0.22, 0.18)
    return jnp.clip(drawn, -bound, bound).astype(kind)


def setup_inputs(seed: int = 0, part: int = 0) -> dict:
    seeds = jax.random.split(jax.random.key(seed), 13)
    part_keys = jax.random.split(jax.random.fold_in(seeds[12], part), 13)
    resid = draw_resid(jax.random.fold_in(jax.random.fold_in(seeds[12], part), 71), part)
    moe_gain = jnp.clip(1.0 + 0.15 * jax.random.normal(seeds[1], (D,), jnp.float32), 0.25, 1.75).astype(jnp.bfloat16)
    routes_keys = jax.random.split(jax.random.fold_in(part_keys[2], 1), TOKENS // TOK_DEV)
    routes_turns = jax.random.permutation(jax.random.fold_in(part_keys[2], 3), TOKENS // TOK_DEV)
    routes = jax.vmap(lambda own, number: assign_block(jax.random.fold_in(part_keys[2], 2), own, number, TOK_DEV, EXPERTS, 2, CAP, 2))(routes_keys, routes_turns).reshape((TOKENS, 2))
    gate_q = touch_ends(jax.random.randint(part_keys[3], (TOKENS, 2), 16, 256), jax.random.fold_in(part_keys[3], 1), 16, 255).astype(jnp.int32)
    doc_lengths = jax.vmap(lambda own: ragged_sizes(own, NDOC, TOK_DEV, TOK_DEV // 2, 2))(jax.random.split(part_keys[4], N_SECT)).reshape((N_SECT, NDOC)).astype(jnp.int32)
    w_gate = scatter_about(seeds[5], (EXPERTS, D, FF), D ** -0.5, 0.09375, ((0, 4), (2, 4)))
    w_up = scatter_about(seeds[6], (EXPERTS, D, FF), D ** -0.5, 0.09375, ((0, 4), (2, 4)))
    w_down = scatter_about(seeds[7], (EXPERTS, FF, D), FF ** -0.5, 0.09375, ((0, 4), (1, 4)))
    attn_gain = jnp.clip(1.0 + 0.15 * jax.random.normal(seeds[8], (D,), jnp.float32), 0.25, 1.75).astype(jnp.bfloat16)
    w_q = draw_w_q(jax.random.fold_in(seeds[12], 71), part)
    w_k = draw_w_k(jax.random.fold_in(seeds[12], 71), part)
    w_v = scatter_about(seeds[11], (D, KVH * HD), D ** -0.5, 0.09375, ((0, 4), (1, 4)))
    return {"resid": resid, "moe_gain": moe_gain, "routes": routes, "gate_q": gate_q, "doc_lengths": doc_lengths, "w_gate": w_gate, "w_up": w_up, "w_down": w_down, "attn_gain": attn_gain, "w_q": w_q, "w_k": w_k, "w_v": w_v}


def layer_norm(values, gain):
    center = values - lax.optimization_barrier(jnp.mean(values, axis=1, keepdims=True))
    spread = lax.optimization_barrier(jnp.mean(center * center, axis=1, keepdims=True))
    return (center * lax.rsqrt(spread + 1e-05) * gain.astype(jnp.float32)).astype(jnp.bfloat16)

def slot_targets(route_rows, experts, capacity):
    flat = route_rows.reshape(-1)
    onehot = (flat[:, None] == jnp.arange(experts, dtype=jnp.int32)[None, :]).astype(jnp.int32)
    before = jnp.cumsum(onehot, axis=0, dtype=jnp.int32) - onehot
    return flat * capacity + lax.optimization_barrier(jnp.sum(before * onehot, axis=1, dtype=jnp.int32))

def source_rows(targets, experts, capacity):
    count = targets.shape[0]
    filler = jnp.full((experts * capacity,), count, jnp.int32)
    return filler.at[targets].set(jnp.arange(count, dtype=jnp.int32)) // 2

def rotate(values, position, head):
    count = values.shape[0]
    split_heads = values.reshape(count, -1, head)
    half = head // 2
    freqs = jnp.exp(jnp.arange(half, dtype=jnp.float32) * (-2.0 * math.log(10000.0) / head))
    angles = position[:, None, None] * freqs[None, None, :]
    cosine = jnp.cos(angles)
    sine = jnp.sin(angles)
    first = split_heads[:, :, :half]
    second = split_heads[:, :, half:]
    turned = jnp.concatenate([first * cosine - second * sine, second * cosine + first * sine], axis=2)
    return turned.reshape(count, -1)

def attend(query, keys, vals, lengths, head, group):
    count = query.shape[0]
    kv_heads = keys.shape[1] // head
    ends = jnp.cumsum(lengths, dtype=jnp.int32)
    places = jnp.arange(count, dtype=jnp.int32)
    after = (places[:, None] >= ends[None, :]).astype(jnp.int32)
    doc_ids = lax.optimization_barrier(jnp.sum(after, axis=1, dtype=jnp.int32))
    starts = lax.optimization_barrier(jnp.sum(after * lengths[None, :], axis=1, dtype=jnp.int32))
    position = (places - starts).astype(jnp.float32)
    rotated_q = rotate(query, position, head).astype(jnp.bfloat16).reshape(count, kv_heads, group, head)
    rotated_k = rotate(keys, position, head).astype(jnp.bfloat16).reshape(count, kv_heads, head)
    value_heads = vals.reshape(count, kv_heads, head)
    allowed = (doc_ids[:, None] == doc_ids[None, :]) & (places[None, :] <= places[:, None])
    scores = jnp.einsum('tkgd,skd->kgts', rotated_q.astype(jnp.float32), rotated_k.astype(jnp.float32)) * (1.0 / math.sqrt(head))
    scores = jnp.where(allowed[None, None], scores, -jnp.inf)
    highest = lax.optimization_barrier(jnp.max(scores, axis=3, keepdims=True))
    weights = jnp.exp(scores - highest)
    probs = (weights / lax.optimization_barrier(jnp.sum(weights, axis=3, keepdims=True))).astype(jnp.bfloat16)
    mixed = jnp.einsum('kgts,skd->tkgd', probs.astype(jnp.float32), value_heads.astype(jnp.float32))
    return mixed.astype(jnp.bfloat16).reshape(count, -1)

def reference(resid, moe_gain, routes, gate_q, doc_lengths, w_gate, w_up, w_down, attn_gain, w_q, w_k, w_v):
    normed = layer_norm(resid.astype(jnp.float32), moe_gain)
    route_blocks = routes.reshape(N_SECT, TOK_DEV, 2)
    targets = jax.vmap(lambda block: slot_targets(block, EXPERTS, CAP))(route_blocks)
    sources = jax.vmap(lambda target: source_rows(target, EXPERTS, CAP))(targets)
    padded = jnp.concatenate([normed.reshape(N_SECT, TOK_DEV, D), jnp.zeros((N_SECT, 1, D), jnp.bfloat16)], axis=1)
    buffers = jax.vmap(lambda rows, index: rows[index])(padded, sources)
    buffers = buffers.reshape(N_SECT, EXPERTS, CAP, D).transpose(1, 0, 2, 3).reshape(EXPERTS, N_SECT * CAP, D)

    def expert(operands):
        rows, gate_w, up_w, down_w = operands
        gate = jnp.dot(rows, gate_w, preferred_element_type=jnp.float32)
        up = jnp.dot(rows, up_w, preferred_element_type=jnp.float32)
        hidden = (jax.nn.silu(gate) * up).astype(jnp.bfloat16)
        return jnp.dot(hidden, down_w, preferred_element_type=jnp.float32)
    outputs = lax.map(expert, (buffers, w_gate, w_up, w_down))
    outputs = outputs.reshape(EXPERTS, N_SECT, CAP, D).transpose(1, 0, 2, 3).reshape(N_SECT, EXPERTS * CAP, D)
    picked = jax.vmap(lambda rows, index: rows[index])(outputs, targets)
    weights = gate_q.reshape(N_SECT, 2 * TOK_DEV).astype(jnp.float32) / 256.0
    mixture = lax.optimization_barrier(jnp.sum((picked * weights[:, :, None]).reshape(N_SECT, TOK_DEV, 2, D), axis=2)).reshape(TOKENS, D)
    new_resid = (resid.astype(jnp.float32) + mixture).astype(jnp.bfloat16)
    normed_next = layer_norm(new_resid.astype(jnp.float32), attn_gain)
    query = jnp.dot(normed_next, w_q, preferred_element_type=jnp.float32)
    keys = jnp.dot(normed_next, w_k, preferred_element_type=jnp.float32)
    vals = jnp.dot(normed_next, w_v, preferred_element_type=jnp.float32).astype(jnp.bfloat16)

    def block_attention(operands):
        block_q, block_k, block_v, lengths = operands
        return attend(block_q, block_k, block_v, lengths, HD, H // KVH)
    context = lax.map(block_attention, (query.reshape(N_SECT, TOK_DEV, H * HD), keys.reshape(N_SECT, TOK_DEV, KVH * HD), vals.reshape(N_SECT, TOK_DEV, KVH * HD), doc_lengths))
    return (new_resid, context.reshape(TOKENS, H * HD))
```

```python
import functools
import math

import jax
import jax.numpy as jnp
from jax import lax
from jax.experimental import pallas as pl
from jax.experimental.pallas import tpu as pltpu
from jax.sharding import PartitionSpec as P

H = 32
KVH = 8
HD = 128
F32 = jnp.float32
BF16 = jnp.bfloat16


def norm_rows(pieces, gain_ref, block_of, store, rows, step):
    width = sum(p.shape[1] for p in pieces)

    def body(i, carry):
        here = pl.ds(pl.multiple_of(i * step, step), step)
        values = [p[here, :].astype(F32) for p in pieces]
        total = values[0]
        for v in values[1:]:
            total = total + v
        mean = jnp.sum(total, axis=1, keepdims=True) / width
        centered = [v - mean for v in values]
        squares = centered[0] * centered[0]
        for c in centered[1:]:
            squares = squares + c * c
        spread = jnp.sum(squares, axis=1, keepdims=True) / width
        scale = lax.rsqrt(spread + 1e-05)
        for k, c in enumerate(centered):
            gain = gain_ref[block_of(k)].astype(F32)
            store(k, here, (c * scale * gain).astype(BF16))
        return carry

    lax.fori_loop(0, rows // step, body, 0)


def up_body(place_ref, *refs):
    pieces = refs[:8]
    gain_ref, gate_ref, up_ref, out_ref, normed = refs[8:]
    hid = place_ref[1]
    rows, local = pieces[0].shape

    @pl.when(pl.program_id(0) == 0)
    def _():
        for j in range(2):

            def store(k, here, values, j=j):
                where = pl.ds(pl.multiple_of((hid ^ k) * local, local), local)
                normed[pl.ds(pl.multiple_of(j * rows + here.start, 16), here.size), where] = values

            norm_rows(pieces[4 * j : 4 * j + 4], gain_ref, lambda k: hid ^ k, store, rows, 16)

    lhs = normed[...]
    gate = jnp.dot(lhs, gate_ref[...], preferred_element_type=F32)
    up = jnp.dot(lhs, up_ref[...], preferred_element_type=F32)
    out_ref[...] = (gate / (1.0 + jnp.exp(-gate)) * up).astype(BF16)


def up_call(place, pieces, gain, gate_w, up_w):
    rows, local = pieces[0].shape
    width, units = gate_w.shape
    block = 256
    whole = pl.BlockSpec((rows, local), lambda i, p: (0, 0))
    weight = pl.BlockSpec((width, block), lambda i, p: (0, i))
    return pl.pallas_call(
        up_body,
        grid_spec=pltpu.PrefetchScalarGridSpec(
            num_scalar_prefetch=1,
            grid=(units // block,),
            in_specs=[whole] * 8
            + [pl.BlockSpec((4, 1, local), lambda i, p: (0, 0, 0)), weight, weight],
            out_specs=pl.BlockSpec((2 * rows, block), lambda i, p: (0, i)),
            scratch_shapes=[pltpu.VMEM((2 * rows, width), BF16)],
        ),
        out_shape=jax.ShapeDtypeStruct((2 * rows, units), BF16),
        compiler_params=pltpu.CompilerParams(
            dimension_semantics=("arbitrary",), vmem_limit_bytes=40 << 20
        ),
        name="up",
    )(place, *pieces, gain, gate_w, up_w)


def down_body(first, place_ref, hidden_ref, down_ref, share_ref, keep_ref, send_ref):
    rows = keep_ref.shape[1]
    out = jnp.dot(hidden_ref[...], down_ref[...], preferred_element_type=F32)
    share = share_ref[...]
    for i in range(out.shape[1] // 128):
        cols = slice(i * 128, (i + 1) * 128)
        scaled = out[:, cols] * share
        keep_ref[0, :, cols] = scaled[:rows]
        send_ref[0, :, cols] = scaled[rows:].astype(BF16)


def down_call(place, hidden, down_w, share, first, count):
    both, units = hidden.shape
    rows = both // 2
    local = down_w.shape[1] // 4
    piece = pl.BlockSpec((1, rows, local), lambda i, p: (i, 0, 0))
    return pl.pallas_call(
        functools.partial(down_body, first),
        grid_spec=pltpu.PrefetchScalarGridSpec(
            num_scalar_prefetch=1,
            grid=(count,),
            in_specs=[
                pl.BlockSpec((both, units), lambda i, p: (0, 0)),
                pl.BlockSpec((units, local), lambda i, p: (0, p[1] ^ (i + first))),
                pl.BlockSpec((both, 128), lambda i, p: (0, 0)),
            ],
            out_specs=[piece, piece],
        ),
        out_shape=[
            jax.ShapeDtypeStruct((count, rows, local), F32),
            jax.ShapeDtypeStruct((count, rows, local), BF16),
        ],
        compiler_params=pltpu.CompilerParams(
            dimension_semantics=("arbitrary",), vmem_limit_bytes=40 << 20
        ),
        name="down",
    )(place, hidden, down_w, share)


def attend_body(place_ref, *refs):
    pieces = refs[:4]
    gain_ref, cos_ref, sin_ref, bias_ref = refs[4:8]
    sources = refs[8:14]
    out_ref = refs[14]
    normed = refs[15]
    buffers = refs[16:22]
    sems = refs[22]
    rows, local = pieces[0].shape
    half = local // 2
    group, hid, sect = place_ref[0], place_ref[1], place_ref[2]
    copies = [
        pltpu.make_async_copy(src, dst, sems.at[i])
        for i, (src, dst) in enumerate(zip(sources, buffers))
    ]
    for c in copies:
        c.start()

    def store(k, here, values):
        normed[2 * (hid ^ k), here, :] = values[:, :half]
        normed[2 * (hid ^ k) + 1, here, :] = values[:, half:]

    norm_rows(pieces, gain_ref, lambda k: hid ^ k, store, rows, 16)
    total = None
    for i in range(6):
        copies[i].wait()
        if i < 2:
            base = 2 * (sect ^ i)
            parts = [(base, slice(0, half)), (base + 1, slice(half, 2 * half))]
        else:
            which = group if i % 2 == 0 else 1 - group
            parts = [(2 * (sect ^ (2 if i < 4 else 3)) + which, slice(0, half))]
        for at, where in parts:
            term = jnp.dot(normed[at], buffers[i][where, :], preferred_element_type=F32)
            total = term if total is None else total + term
    heads = local // HD
    kv_heads = (total.shape[1] - local) // (2 * HD)
    cos, sin, bias = cos_ref[...], sin_ref[...], bias_ref[...]

    def turned(x):
        return (x * cos + pltpu.roll(x, HD // 2, 1) * sin).astype(BF16)

    for g in range(kv_heads):
        key = turned(total[:, local + g * HD : local + (g + 1) * HD])
        at = local + (kv_heads + g) * HD
        val = total[:, at : at + HD].astype(BF16)
        for r in range(heads // kv_heads):
            cols = slice((g * (heads // kv_heads) + r) * HD, (g * (heads // kv_heads) + r + 1) * HD)
            query = turned(total[:, cols])
            scores = lax.dot_general(
                query, key, (((1,), (1,)), ((), ())), preferred_element_type=F32
            ) * (1.0 / math.sqrt(HD)) + bias
            weights = jnp.exp(scores - jnp.max(scores, axis=1, keepdims=True))
            probs = (weights / jnp.sum(weights, axis=1, keepdims=True)).astype(BF16)
            out_ref[:, cols] = jnp.dot(probs, val, preferred_element_type=F32).astype(BF16)


def attend_call(place, pieces, gain, cos, sin, bias, weights):
    rows, local = pieces[0].shape
    vmem = pl.BlockSpec(memory_space=pltpu.VMEM)
    return pl.pallas_call(
        attend_body,
        in_specs=[pl.BlockSpec(memory_space=pltpu.SMEM)]
        + [vmem] * 8
        + [pl.BlockSpec(memory_space=pl.ANY)] * 6,
        out_specs=vmem,
        out_shape=jax.ShapeDtypeStruct((rows, local), BF16),
        scratch_shapes=[pltpu.VMEM((8, rows, local // 2), BF16)]
        + [pltpu.VMEM(w.shape, BF16) for w in weights]
        + [pltpu.SemaphoreType.DMA((6,))],
        compiler_params=pltpu.CompilerParams(vmem_limit_bytes=40 << 20),
        name="attend",
    )(place, *pieces, gain, cos, sin, bias, *weights)


def swap(value, axis, size, by):
    return lax.ppermute(value, axis, [(i, i ^ by) for i in range(size)])


def position_tables(lengths, count):
    ends = jnp.cumsum(lengths, dtype=jnp.int32)
    places = jnp.arange(count, dtype=jnp.int32)
    after = (places[:, None] >= ends[None, :]).astype(jnp.int32)
    doc_ids = jnp.sum(after, axis=1, dtype=jnp.int32)
    starts = jnp.sum(after * lengths[None, :], axis=1, dtype=jnp.int32)
    position = (places - starts).astype(F32)
    half = HD // 2
    freqs = jnp.exp(jnp.arange(half, dtype=F32) * (-2.0 * math.log(10000.0) / HD))
    angles = position[:, None] * freqs[None, :]
    cosine = jnp.cos(angles)
    sine = jnp.sin(angles)
    allowed = (doc_ids[:, None] == doc_ids[None, :]) & (places[None, :] <= places[:, None])
    bias = jnp.where(allowed, 0.0, -jnp.inf).astype(F32)
    return (
        jnp.concatenate([cosine, cosine], axis=1),
        jnp.concatenate([-sine, sine], axis=1),
        bias,
    )


def on_grid(
    resid, moe_gain, routes, gate_q, doc_lengths, w_gate, w_up, w_down, attn_gain, w_q, w_k, w_v
):
    tokens, local = resid.shape
    group = lax.axis_index("groups")
    sect = lax.axis_index("sect")
    hid = lax.axis_index("hid")
    place = jnp.stack([group, hid, sect]).astype(jnp.int32)

    over_hid = lambda v, by: swap(v, "hid", 4, by)
    over_core = lambda v: swap(v, "sect", 4, 1)
    over_chip = lambda v: swap(v, "sect", 4, 2)
    over_group = lambda v: swap(v, "groups", 2, 1)

    own = [resid, over_hid(resid, 1), over_hid(resid, 2), over_hid(resid, 3)]
    own_pair = own + [over_core(v) for v in own]
    far = [over_chip(v) for v in own]
    far_pair = far + [over_core(v) for v in far]

    weights = gate_q.astype(F32) / 256.0
    shares = []
    for j in range(4):
        mine = jnp.sum(jnp.where(routes == (sect ^ j), weights, 0.0), axis=1).reshape(1, tokens)
        shares.append(mine if j == 0 else swap(mine, "sect", 4, j))
    wide = [jnp.broadcast_to(v.reshape(tokens, 1), (tokens, 128)) for v in shares]
    near_share = jnp.concatenate(wide[:2], axis=0)
    far_share = jnp.concatenate(wide[2:], axis=0)

    w_all = jnp.concatenate([w_q, w_k, w_v], axis=1)
    w_half = lax.dynamic_slice_in_dim(w_all, group * (local // 2), local // 2, axis=0)
    w_far = over_chip(w_half)
    w_far_other = over_group(w_far)
    proj = [w_all, over_core(w_all), w_far, w_far_other, over_core(w_far), over_core(w_far_other)]

    gain = moe_gain.reshape(4, 1, local)
    hidden = up_call(place, own_pair, gain, w_gate[0], w_up[0])
    near_keep, near_send = down_call(place, hidden, w_down[0], near_share, 0, 4)
    near_got = over_core(near_send)
    near = near_keep + near_got.astype(F32)

    hidden_far = up_call(place, far_pair, gain, w_gate[0], w_up[0])
    parts = [None] * 4
    for k in (3, 2, 1, 0):
        keep, send = down_call(place, hidden_far, w_down[0], far_share, k, 1)
        summed = (keep[0] + over_core(send[0]).astype(F32)).astype(BF16)
        part = near[k] + over_chip(summed).astype(F32)
        parts[k] = part if k == 0 else over_hid(part.astype(BF16), k)
    mixture = parts[0]
    for k in (1, 2, 3):
        mixture = mixture + parts[k].astype(F32)
    new_local = (resid.astype(F32) + mixture).astype(BF16)

    rows = [new_local, over_hid(new_local, 1), over_hid(new_local, 2), over_hid(new_local, 3)]
    cos, sin, bias = position_tables(doc_lengths[0], tokens)
    context = attend_call(place, rows, attn_gain.reshape(4, 1, local), cos, sin, bias, proj)
    return (new_local, context)


def layer_norm(values, gain):
    center = values - jnp.mean(values, axis=1, keepdims=True)
    spread = jnp.mean(center * center, axis=1, keepdims=True)
    return (center * lax.rsqrt(spread + 1e-05) * gain.astype(jnp.float32)).astype(jnp.bfloat16)


def slot_targets(route_rows, experts, capacity):
    flat = route_rows.reshape(-1)
    onehot = (flat[:, None] == jnp.arange(experts, dtype=jnp.int32)[None, :]).astype(jnp.int32)
    before = jnp.cumsum(onehot, axis=0, dtype=jnp.int32) - onehot
    return flat * capacity + jnp.sum(before * onehot, axis=1, dtype=jnp.int32)


def source_rows(targets, experts, capacity):
    count = targets.shape[0]
    filler = jnp.full((experts * capacity,), count, jnp.int32)
    return filler.at[targets].set(jnp.arange(count, dtype=jnp.int32)) // 2


def rotate(values, position, head):
    count = values.shape[0]
    split_heads = values.reshape(count, -1, head)
    half = head // 2
    freqs = jnp.exp(jnp.arange(half, dtype=jnp.float32) * (-2.0 * math.log(10000.0) / head))
    angles = position[:, None, None] * freqs[None, None, :]
    cosine = jnp.cos(angles)
    sine = jnp.sin(angles)
    first = split_heads[:, :, :half]
    second = split_heads[:, :, half:]
    turned = jnp.concatenate(
        [first * cosine - second * sine, second * cosine + first * sine], axis=2
    )
    return turned.reshape(count, -1)


def attend(query, keys, vals, lengths, head, group):
    count = query.shape[0]
    kv_heads = keys.shape[1] // head
    ends = jnp.cumsum(lengths, dtype=jnp.int32)
    places = jnp.arange(count, dtype=jnp.int32)
    after = (places[:, None] >= ends[None, :]).astype(jnp.int32)
    doc_ids = jnp.sum(after, axis=1, dtype=jnp.int32)
    starts = jnp.sum(after * lengths[None, :], axis=1, dtype=jnp.int32)
    position = (places - starts).astype(jnp.float32)
    rotated_q = (
        rotate(query, position, head).astype(jnp.bfloat16).reshape(count, kv_heads, group, head)
    )
    rotated_k = rotate(keys, position, head).astype(jnp.bfloat16).reshape(count, kv_heads, head)
    value_heads = vals.reshape(count, kv_heads, head)
    allowed = (doc_ids[:, None] == doc_ids[None, :]) & (places[None, :] <= places[:, None])
    scores = jnp.einsum(
        "tkgd,skd->kgts", rotated_q, rotated_k, preferred_element_type=jnp.float32
    ) * (1.0 / math.sqrt(head))
    scores = jnp.where(allowed[None, None], scores, -jnp.inf)
    highest = jnp.max(scores, axis=3, keepdims=True)
    weights = jnp.exp(scores - highest)
    probs = (weights / jnp.sum(weights, axis=3, keepdims=True)).astype(jnp.bfloat16)
    mixed = jnp.einsum("kgts,skd->tkgd", probs, value_heads, preferred_element_type=jnp.float32)
    return mixed.astype(jnp.bfloat16).reshape(count, -1)


def on_device(
    resid, moe_gain, routes, gate_q, doc_lengths, w_gate, w_up, w_down, attn_gain, w_q, w_k, w_v
):
    sections = lax.axis_size("sect")
    slices = lax.axis_size("hid")
    tokens_here, local_width = resid.shape
    width = local_width * slices
    capacity = 4 * tokens_here // sections
    entry = lax.all_gather(resid, "hid", axis=1, tiled=True)
    normed = layer_norm(entry.astype(jnp.float32), moe_gain)
    targets = slot_targets(routes, sections, capacity)
    sources = source_rows(targets, sections, capacity)
    padded = jnp.concatenate([normed, jnp.zeros((1, width), jnp.bfloat16)], axis=0)
    gate_w = w_gate[0]
    up_w = w_up[0]
    down_w = w_down[0]
    outgoing = padded[sources].reshape(sections, capacity, width)
    arrived = lax.all_to_all(outgoing, "sect", split_axis=0, concat_axis=0, tiled=True).reshape(
        sections * capacity, width
    )
    gate = jnp.dot(arrived, gate_w, preferred_element_type=jnp.float32)
    up = jnp.dot(arrived, up_w, preferred_element_type=jnp.float32)
    hidden = (jax.nn.silu(gate) * up).astype(jnp.bfloat16)
    weights = gate_q.reshape(-1).astype(jnp.float32) / 256.0
    own_resid = resid.astype(jnp.float32)
    outputs = jnp.dot(hidden, down_w, preferred_element_type=jnp.float32)
    mine = lax.psum_scatter(outputs, "hid", scatter_dimension=1, tiled=True)
    returned = lax.all_to_all(
        mine.reshape(sections, capacity, local_width),
        "sect",
        split_axis=0,
        concat_axis=0,
        tiled=True,
    )
    picked = returned.reshape(sections * capacity, local_width)[targets]
    mixture = jnp.sum((picked * weights[:, None]).reshape(tokens_here, 2, local_width), axis=1)
    new_local = (own_resid + mixture).astype(jnp.bfloat16)
    full_rows = lax.all_gather(new_local, "hid", axis=1, tiled=True)
    normed_next = layer_norm(full_rows.astype(jnp.float32), attn_gain)
    query = jnp.dot(
        normed_next,
        lax.all_gather(w_q, "sect", axis=0, tiled=True),
        preferred_element_type=jnp.float32,
    )
    keys = jnp.dot(
        normed_next,
        lax.all_gather(w_k, "sect", axis=0, tiled=True),
        preferred_element_type=jnp.float32,
    )
    vals = jnp.dot(
        normed_next,
        lax.all_gather(w_v, "sect", axis=0, tiled=True),
        preferred_element_type=jnp.float32,
    )
    context = attend(query, keys, vals.astype(jnp.bfloat16), doc_lengths[0], HD, H // KVH)
    return (new_local, context)


def solution(mesh):
    in_specs = (
        P(("groups", "sect"), "hid"),
        P(),
        P(("groups", "sect"), None),
        P(("groups", "sect"), None),
        P(("groups", "sect"), None),
        P("sect", None, "hid"),
        P("sect", None, "hid"),
        P("sect", "hid", None),
        P(),
        P("sect", "hid"),
        P("sect", "hid"),
        P("sect", "hid"),
    )
    out_specs = (P(("groups", "sect"), "hid"), P(("groups", "sect"), "hid"))
    plan = on_device
    if dict(mesh.shape) == {"groups": 2, "sect": 4, "hid": 4}:
        plan = on_grid
    return jax.shard_map(
        plan, mesh=mesh, in_specs=in_specs, out_specs=out_specs, check_vma=False
    )
```

```python
import math

import jax
import jax.numpy as jnp
from jax import lax
from jax.experimental import pallas as pl
from jax.experimental.pallas import tpu as pltpu
from jax.sharding import PartitionSpec as P

H = 32
KVH = 8
HD = 128
F32 = jnp.float32
BF16 = jnp.bfloat16
LIMIT = 16
SLOTS = 4
DEEP = 1024
ORDER = (3, 1, 2, 0)
TINY = pl.CostEstimate(flops=1, transcendentals=0, bytes_accessed=1)
STEP = pl.CostEstimate(flops=1 << 22, transcendentals=0, bytes_accessed=1 << 10)
VMEM = pl.BlockSpec(memory_space=pltpu.VMEM)
SMEM = pl.BlockSpec(memory_space=pltpu.SMEM)


def reads(count):
    return pl.CostEstimate(flops=1, transcendentals=0, bytes_accessed=count)


def features(piece):
    return pl.BlockSpec((piece.shape[0], piece.shape[1] // 1024 * 1024), lambda *_: (0, 0))


def routing(piece):
    return pl.BlockSpec((piece.shape[0], 128), lambda *_: (0, piece.shape[1] // 128 - 1))


def whole(shape):
    return pl.BlockSpec(shape, lambda *_: (0,) * len(shape))


def stats_body(before, first_ref, *refs):
    pieces = [first_ref] + list(refs[:-4]) if before else [first_ref] + list(refs[:-2])
    rows, local = first_ref.shape
    mean_ref, spread_ref = refs[-2], refs[-1]
    for j, p in enumerate(pieces):
        here = slice(j * rows, (j + 1) * rows)
        values = p[...].astype(F32)
        mean = jnp.sum(values, axis=1, keepdims=True) / local
        values = values - mean
        spread = jnp.sum(values * values, axis=1, keepdims=True)
        if before:
            seen = before * local
            old = refs[-4][here, :]
            gap = mean - old
            spread = refs[-3][here, :] + spread + gap * gap * (seen * local / (seen + local))
            mean = old + gap * (local / (seen + local))
        mean_ref[here, :] = mean
        spread_ref[here, :] = spread


def stats_call(pieces, seen, before, cost, name):
    rows = sum(p.shape[0] for p in pieces)
    operands = list(pieces) + list(before or ())
    return pl.pallas_call(
        lambda *refs: stats_body(seen, *refs),
        grid=(1,),
        in_specs=[features(v) for v in pieces] + [whole(v.shape) for v in before or ()],
        out_specs=[whole((rows, 1))] * 2,
        out_shape=[jax.ShapeDtypeStruct((rows, 1), F32)] * 2,
        compiler_params=pltpu.CompilerParams(vmem_limit_bytes=LIMIT << 20),
        cost_estimate=cost,
        name=name,
    )(*operands)


def stats_chain(groups, name):
    before = None
    for seen, pieces in enumerate(groups):
        before = list(stats_call(pieces, seen, before, STEP, name))
    return before


def full_norm_rows(pieces, gain_ref, hid, out_ref, first, step):
    rows, local = pieces[0].shape
    width = local * len(pieces)

    def body(i, carry):
        at = pl.multiple_of(i * step, step)
        values = [p[pl.ds(at, step), :].astype(F32) for p in pieces]
        total = values[0]
        for v in values[1:]:
            total = total + v
        mean = jnp.sum(total, axis=1, keepdims=True) / width
        centered = [v - mean for v in values]
        squares = centered[0] * centered[0]
        for c in centered[1:]:
            squares = squares + c * c
        spread = jnp.sum(squares, axis=1, keepdims=True) / width
        scale = lax.rsqrt(spread + 1e-05)
        for k, c in enumerate(centered):
            cols = pl.ds(pl.multiple_of((hid ^ k) * local, local), local)
            gain = gain_ref[:, cols].astype(F32)
            out_ref[pl.ds(first + at, step), cols] = (c * scale * gain).astype(BF16)
        return carry

    lax.fori_loop(0, rows // step, body, 0)


def norm_rows(pieces, gain_ref, mean_ref, spread_ref, hid, out_ref, first, step):
    rows, local = pieces[0].shape
    width = local * len(pieces)
    for k, p in enumerate(pieces):
        cols = pl.ds(pl.multiple_of((hid ^ k) * local, local), local)
        gain = gain_ref[:, cols].astype(F32)
        for at in range(0, rows, step):
            here = slice(first + at, first + at + step)
            scale = lax.rsqrt(spread_ref[here, :] / width + 1e-05)
            values = p[at : at + step, :].astype(F32) - mean_ref[here, :]
            out_ref[here, cols] = (values * scale * gain).astype(BF16)


def expert_body(place_ref, *refs):
    pieces = refs[:8]
    gain_ref, gate_hbm, up_hbm, down_hbm = refs[8:12]
    routed, keep_ref, send_ref = refs[12:14], refs[14], refs[15]
    normed, sums, hidden, ring, sems = refs[16:]
    rows, local = pieces[1].shape
    slots, deep = ring.shape[:2]
    width, units = gate_hbm.shape
    ups = 2 * (width // deep)
    hid, sect = place_ref[1], place_ref[2]

    def copy(n):
        if n < ups:
            src = (gate_hbm, up_hbm)[n % 2].at[n // 2 * deep : (n // 2 + 1) * deep, :]
        else:
            at = pl.multiple_of((hid ^ ORDER[n - ups]) * local, local)
            src = down_hbm.at[:, pl.ds(at, local)]
        return pltpu.make_async_copy(src, ring.at[n % slots], sems.at[n % slots])

    for n in range(slots):
        copy(n).start()
    for j in range(2):
        mine = pieces[4 * j : 4 * j + 4]
        full_norm_rows(mine, gain_ref, hid, normed, j * rows, 64)
    shares = []
    for ref in routed:
        chosen = lax.broadcasted_iota(jnp.int32, ref.shape, 1) == sect
        units_of = jnp.sum(jnp.where(chosen, ref[...].astype(F32), 0.0), axis=1, keepdims=True)
        shares.append(units_of / 256.0)
    for n in range(ups + 4):
        copy(n).wait()
        if n < ups:
            lhs = normed[:, n // 2 * deep : (n // 2 + 1) * deep]
            term = jnp.dot(lhs, ring[n % slots], preferred_element_type=F32)
            sums[n % 2] = term if n < 2 else sums[n % 2] + term
        else:
            if n == ups:
                for b in range(0, units, 128):
                    gate = sums[0, :, b : b + 128]
                    up = sums[1, :, b : b + 128]
                    hidden[:, b : b + 128] = (gate / (1.0 + jnp.exp(-gate)) * up).astype(BF16)
            out = jnp.dot(hidden[...], ring[n % slots], preferred_element_type=F32)
            keep_ref[n - ups] = out[:rows] * shares[0]
            send_ref[n - ups] = (out[rows:] * shares[1]).astype(BF16)
        if n + slots < ups + 4:
            copy(n + slots).start()


def expert_call(place, pieces, gain, gate_w, up_w, down_w, name):
    rows, local = pieces[1].shape
    width, units = gate_w.shape
    once = pl.Buffered(1)
    held = [pl.BlockSpec((rows, local), lambda *_: (0, 0), pipeline_mode=once)] * 8
    pieces = [pltpu.with_memory_space_constraint(p, pltpu.HBM) for p in pieces]
    routed = [pieces[0], pieces[4]]
    shape = (4, rows, local)
    return pl.pallas_call(
        expert_body,
        grid=(1,),
        in_specs=[SMEM]
        + held
        + [whole(gain.shape)]
        + [pl.BlockSpec(memory_space=pl.ANY)] * 3
        + [routing(v) for v in routed],
        out_specs=[whole(shape)] * 2,
        out_shape=[jax.ShapeDtypeStruct(shape, F32), jax.ShapeDtypeStruct(shape, BF16)],
        scratch_shapes=[
            pltpu.VMEM((2 * rows, width), BF16),
            pltpu.VMEM((2, 2 * rows, units), F32),
            pltpu.VMEM((2 * rows, units), BF16),
            pltpu.VMEM((SLOTS, DEEP, units), BF16),
            pltpu.SemaphoreType.DMA((SLOTS,)),
        ],
        compiler_params=pltpu.CompilerParams(vmem_limit_bytes=26 << 20),
        cost_estimate=TINY,
        name=name,
    )(place, *pieces, gain, gate_w, up_w, down_w, *routed)


def sums_call(body, operands, outs, name):
    return pl.pallas_call(
        body,
        grid=(1,),
        in_specs=[whole(v.shape) for v in operands],
        out_specs=[whole(shape) for shape, _ in outs],
        out_shape=[jax.ShapeDtypeStruct(*o) for o in outs],
        compiler_params=pltpu.CompilerParams(vmem_limit_bytes=LIMIT << 20),
        cost_estimate=TINY,
        name=name,
    )(*operands)


def core_body(keep_ref, got_ref, first_ref, second_ref):
    for n in range(4):
        out_ref = (first_ref, second_ref)[n // 2]
        out_ref[n % 2] = (keep_ref[n] + got_ref[n].astype(F32)).astype(BF16)


def chip_body(keep_ref, near_ref, far_ref, out_ref):
    for n in range(2):
        total = keep_ref[n] + near_ref[n].astype(F32) + far_ref[n].astype(F32)
        out_ref[n] = total.astype(BF16)


def pair_body(keep_ref, near_ref, far_ref, hid_ref, resid_ref, send_ref, own_ref):
    both = []
    for n in range(2):
        total = keep_ref[n + 2] + near_ref[n + 2].astype(F32) + far_ref[n].astype(F32)
        both.append(total + hid_ref[n].astype(F32))
    send_ref[...] = both[0].astype(BF16)
    own_ref[...] = resid_ref[...].astype(F32) + both[1]


def last_body(own_ref, got_ref, out_ref):
    out_ref[...] = (own_ref[...] + got_ref[...].astype(F32)).astype(BF16)


def attend_body(place_ref, *refs):
    pieces = refs[:4]
    mean_ref, spread_ref, gain_ref, cos_ref, sin_ref, bias_ref = refs[4:10]
    sources = refs[10:26]
    out_ref, normed, total = refs[26:29]
    weights = refs[29:45]
    sems = refs[45]
    rows, local = pieces[0].shape
    half = local // 2
    group, hid, sect = place_ref[0], place_ref[1], place_ref[2]
    copies = [
        pltpu.make_async_copy(src, dst, sems.at[i])
        for i, (src, dst) in enumerate(zip(sources, weights))
    ]
    for c in copies:
        c.start()
    norm_rows(pieces, gain_ref, mean_ref, spread_ref, hid, normed, 0, 64)

    def rows_of(at, count):
        return normed[:, pl.ds(pl.multiple_of(at, 512), count)]

    starts = [(sect ^ j) * local for j in range(4)]
    mine, other = group * half, (1 - group) * half
    halves = [rows_of(starts[j] + o, half) for j in (2, 3) for o in (mine, other)]
    wholes = [rows_of(at, local) for at in starts]
    plan = []
    for c in range(2):
        cols = slice(c * half, (c + 1) * half)
        plan.append([(wholes[i], i, cols) for i in range(2)])
        plan[c] += [(halves[i], 2 + 4 * c + i, slice(0, half)) for i in range(4)]
    plan.append([(wholes[i], 10 + i, slice(0, half)) for i in range(2)])
    plan[2] += [(halves[i], 12 + i, slice(0, half)) for i in range(4)]
    waited = set()
    for c, terms in enumerate(plan):
        acc = None
        for lhs, n, cols in terms:
            if n not in waited:
                copies[n].wait()
                waited.add(n)
            term = jnp.dot(lhs, weights[n][:, cols], preferred_element_type=F32)
            acc = term if acc is None else acc + term
        total[:, c * half : (c + 1) * half] = acc
    heads = local // HD
    kv_heads = (total.shape[1] - local) // (2 * HD)
    cos, sin, bias = cos_ref[...], sin_ref[...], bias_ref[...]

    def turned(at):
        x = total[:, at : at + HD]
        return (x * cos + pltpu.roll(x, HD // 2, 1) * sin).astype(BF16)

    for g in range(kv_heads):
        key = turned(local + g * HD)
        at = local + (kv_heads + g) * HD
        val = total[:, at : at + HD].astype(BF16)
        for r in range(heads // kv_heads):
            at = (g * (heads // kv_heads) + r) * HD
            scores = lax.dot_general(
                turned(at), key, (((1,), (1,)), ((), ())), preferred_element_type=F32
            ) * (1.0 / math.sqrt(HD)) + bias
            weight = jnp.exp(scores - jnp.max(scores, axis=1, keepdims=True))
            probs = (weight / jnp.sum(weight, axis=1, keepdims=True)).astype(BF16)
            mixed = jnp.dot(probs, val, preferred_element_type=F32)
            out_ref[:, at : at + HD] = mixed.astype(BF16)


def attend_call(place, pieces, stats, gain, cos, sin, bias, weights):
    rows, local = pieces[0].shape
    return pl.pallas_call(
        attend_body,
        grid=(1,),
        in_specs=[SMEM]
        + [whole(v.shape) for v in (*pieces, *stats, gain, cos, sin, bias)]
        + [pl.BlockSpec(memory_space=pl.ANY)] * len(weights),
        out_specs=whole((rows, local)),
        out_shape=jax.ShapeDtypeStruct((rows, local), BF16),
        scratch_shapes=[pltpu.VMEM((rows, 4 * local), BF16), pltpu.VMEM((rows, 3 * local // 2), F32)]
        + [pltpu.VMEM(w.shape, BF16) for w in weights]
        + [pltpu.SemaphoreType.DMA((len(weights),))],
        compiler_params=pltpu.CompilerParams(vmem_limit_bytes=20 << 20),
        cost_estimate=TINY,
        name="attend",
    )(place, *pieces, *stats, gain, cos, sin, bias, *weights)


def swap(value, axis, size, by):
    return lax.ppermute(value, axis, [(i, i ^ by) for i in range(size)])


def tie(*values):
    return lax.optimization_barrier(values)


def position_tables(lengths, count):
    ends = jnp.cumsum(lengths, dtype=jnp.int32)
    places = jnp.arange(count, dtype=jnp.int32)
    past = (places[:, None] >= ends[None, :]).astype(jnp.int32)
    doc_ids = jnp.sum(past, axis=1, dtype=jnp.int32)
    starts = jnp.sum(past * lengths[None, :], axis=1, dtype=jnp.int32)
    position = (places - starts).astype(F32)
    half = HD // 2
    freqs = jnp.exp(jnp.arange(half, dtype=F32) * (-2.0 * math.log(10000.0) / HD))
    angles = position[:, None] * freqs[None, :]
    cosine = jnp.cos(angles)
    sine = jnp.sin(angles)
    allowed = (doc_ids[:, None] == doc_ids[None, :]) & (places[None, :] <= places[:, None])
    bias = jnp.where(allowed, 0.0, -jnp.inf).astype(F32)
    return (
        jnp.concatenate([cosine, cosine], axis=1),
        jnp.concatenate([-sine, sine], axis=1),
        bias,
    )


def on_grid(
    resid, moe_gain, routes, gate_q, doc_lengths, w_gate, w_up, w_down, attn_gain, w_q, w_k, w_v
):
    tokens, local = resid.shape
    half = local // 2
    group = lax.axis_index("groups")
    sect = lax.axis_index("sect")
    hid = lax.axis_index("hid")
    place = jnp.stack([group, hid, sect]).astype(jnp.int32)

    over_hid = lambda v, by: swap(v, "hid", 4, by)
    over_core = lambda v: swap(v, "sect", 4, 1)
    over_chip = lambda v: swap(v, "sect", 4, 2)
    over_group = lambda v: swap(v, "groups", 2, 1)

    def half_of(w, c):
        return lax.dynamic_slice(w, (group * half, c * half), (half, half))

    here, there, here_core, there_core = ([None] * 3 for _ in range(4))
    gate_w, up_w, down_w = (
        pltpu.with_memory_space_constraint(w[0], pltpu.HBM) for w in (w_gate, w_up, w_down)
    )

    first, second, third = (over_hid(resid, k) for k in (1, 2, 3))
    experts = jnp.arange(128, dtype=jnp.int32)
    units = jnp.sum(jnp.where(routes[:, :, None] == experts, gate_q[:, :, None], 0), axis=1)
    marked = jnp.concatenate([resid, units.astype(BF16)], axis=1)
    far_own = over_chip(marked)
    here[0] = over_chip(half_of(w_q, 0))
    w_kv = jnp.concatenate([w_k, w_v], axis=1)
    waiting = [half_of(w_q, 1), half_of(w_kv, 0)]
    tables = position_tables(doc_lengths[0], tokens)
    first, second, far_own, here[0], marked, w_q, w_kv, *held = tie(
        first, second, far_own, here[0], marked, w_q, w_kv, *waiting, *tables
    )
    waiting, tables = held[:2], held[2:]
    near = [marked, first, second, third]
    near_pair = [over_core(v) for v in near]
    far = [far_own] + [over_chip(v) for v in near[1:]]

    gain = moe_gain.reshape(1, -1)
    weights = (gate_w, up_w, down_w)
    near_keep, near_send = expert_call(place, near + near_pair, gain, *weights, "near")
    near_send, *far = tie(near_send, *far)
    far[3], waiting[0] = tie(far[3], waiting[0])
    here[1] = over_chip(waiting[0])
    far_pair = [over_core(v) for v in far]
    far_keep, far_send = expert_call(place, far + far_pair, gain, *weights, "far")
    far_send, near_send, here[0], here[1] = tie(far_send, near_send, here[0], here[1])

    rows_of = (2, tokens, local)
    near_got, there[0] = over_core(near_send), over_group(here[0])
    operands = [far_keep, over_core(far_send)]
    summed = list(sums_call(core_body, operands, [(rows_of, BF16)] * 2, "sum_core"))
    got = over_chip(summed[0])
    got, near_got, there[0], here[0], here[1], summed[1] = tie(
        got, near_got, there[0], here[0], here[1], summed[1]
    )
    got_rest, there[1] = over_chip(summed[1]), over_group(here[1])
    here_core[0], there_core[0] = over_core(here[0]), over_core(there[0])
    operands = [near_keep, near_got, got]
    (part,) = sums_call(chip_body, operands, [(rows_of, BF16)], "sum_chip")
    part = over_hid(part, 1)
    part, got_rest, there[1], here_core[0], there_core[0], here[1], w_q, waiting[1] = tie(
        part, got_rest, there[1], here_core[0], there_core[0], here[1], w_q, waiting[1]
    )
    here[2], q_near = over_chip(waiting[1]), over_core(w_q)
    here_core[1], there_core[1] = over_core(here[1]), over_core(there[1])
    operands = [near_keep, near_got, got_rest, part, resid]
    one = (tokens, local)
    send, own = sums_call(pair_body, operands, [(one, BF16), (one, F32)], "sum_pair")
    send = over_hid(send, 2)
    send, here[2], q_near, here_core[1], there_core[1], w_kv = tie(
        send, here[2], q_near, here_core[1], there_core[1], w_kv
    )
    (new_local,) = sums_call(last_body, [own, send], [(one, BF16)], "sum_hid")

    there[2], here_core[2], kv_near = over_group(here[2]), over_core(here[2]), over_core(w_kv)
    rows = [new_local, over_hid(new_local, 1), over_hid(new_local, 2), None]
    rows[1], rows[2], there[2], here_core[2], kv_near = tie(
        rows[1], rows[2], there[2], here_core[2], kv_near
    )
    rows[3], there_core[2] = over_hid(rows[2], 1), over_core(there[2])
    moved = [(here[c], there[c], here_core[c], there_core[c]) for c in range(3)]
    proj = [w_q, q_near, *moved[0], *moved[1], w_kv, kv_near, *moved[2]]
    stats = stats_chain([[r] for r in rows], "stats_next")
    gain = attn_gain.reshape(1, -1)
    context = attend_call(place, rows, stats, gain, *tables, proj)
    return (new_local, context)


def layer_norm(values, gain):
    center = values - jnp.mean(values, axis=1, keepdims=True)
    spread = jnp.mean(center * center, axis=1, keepdims=True)
    return (center * lax.rsqrt(spread + 1e-05) * gain.astype(jnp.float32)).astype(jnp.bfloat16)


def slot_targets(route_rows, experts, capacity):
    flat = route_rows.reshape(-1)
    onehot = (flat[:, None] == jnp.arange(experts, dtype=jnp.int32)[None, :]).astype(jnp.int32)
    before = jnp.cumsum(onehot, axis=0, dtype=jnp.int32) - onehot
    return flat * capacity + jnp.sum(before * onehot, axis=1, dtype=jnp.int32)


def source_rows(targets, experts, capacity):
    count = targets.shape[0]
    filler = jnp.full((experts * capacity,), count, jnp.int32)
    return filler.at[targets].set(jnp.arange(count, dtype=jnp.int32)) // 2


def rotate(values, position, head):
    count = values.shape[0]
    split_heads = values.reshape(count, -1, head)
    half = head // 2
    freqs = jnp.exp(jnp.arange(half, dtype=jnp.float32) * (-2.0 * math.log(10000.0) / head))
    angles = position[:, None, None] * freqs[None, None, :]
    cosine = jnp.cos(angles)
    sine = jnp.sin(angles)
    first = split_heads[:, :, :half]
    second = split_heads[:, :, half:]
    turned = jnp.concatenate(
        [first * cosine - second * sine, second * cosine + first * sine], axis=2
    )
    return turned.reshape(count, -1)


def attend(query, keys, vals, lengths, head, group):
    count = query.shape[0]
    kv_heads = keys.shape[1] // head
    ends = jnp.cumsum(lengths, dtype=jnp.int32)
    places = jnp.arange(count, dtype=jnp.int32)
    after = (places[:, None] >= ends[None, :]).astype(jnp.int32)
    doc_ids = jnp.sum(after, axis=1, dtype=jnp.int32)
    starts = jnp.sum(after * lengths[None, :], axis=1, dtype=jnp.int32)
    position = (places - starts).astype(jnp.float32)
    rotated_q = (
        rotate(query, position, head).astype(jnp.bfloat16).reshape(count, kv_heads, group, head)
    )
    rotated_k = rotate(keys, position, head).astype(jnp.bfloat16).reshape(count, kv_heads, head)
    value_heads = vals.reshape(count, kv_heads, head)
    allowed = (doc_ids[:, None] == doc_ids[None, :]) & (places[None, :] <= places[:, None])
    scores = jnp.einsum(
        "tkgd,skd->kgts", rotated_q, rotated_k, preferred_element_type=jnp.float32
    ) * (1.0 / math.sqrt(head))
    scores = jnp.where(allowed[None, None], scores, -jnp.inf)
    highest = jnp.max(scores, axis=3, keepdims=True)
    weights = jnp.exp(scores - highest)
    probs = (weights / jnp.sum(weights, axis=3, keepdims=True)).astype(jnp.bfloat16)
    mixed = jnp.einsum("kgts,skd->tkgd", probs, value_heads, preferred_element_type=jnp.float32)
    return mixed.astype(jnp.bfloat16).reshape(count, -1)


def on_device(
    resid, moe_gain, routes, gate_q, doc_lengths, w_gate, w_up, w_down, attn_gain, w_q, w_k, w_v
):
    sections = lax.axis_size("sect")
    slices = lax.axis_size("hid")
    tokens_here, local_width = resid.shape
    width = local_width * slices
    capacity = 4 * tokens_here // sections
    entry = lax.all_gather(resid, "hid", axis=1, tiled=True)
    normed = layer_norm(entry.astype(jnp.float32), moe_gain)
    targets = slot_targets(routes, sections, capacity)
    sources = source_rows(targets, sections, capacity)
    padded = jnp.concatenate([normed, jnp.zeros((1, width), jnp.bfloat16)], axis=0)
    gate_w = w_gate[0]
    up_w = w_up[0]
    down_w = w_down[0]
    outgoing = padded[sources].reshape(sections, capacity, width)
    arrived = lax.all_to_all(outgoing, "sect", split_axis=0, concat_axis=0, tiled=True).reshape(
        sections * capacity, width
    )
    gate = jnp.dot(arrived, gate_w, preferred_element_type=jnp.float32)
    up = jnp.dot(arrived, up_w, preferred_element_type=jnp.float32)
    hidden = (jax.nn.silu(gate) * up).astype(jnp.bfloat16)
    weights = gate_q.reshape(-1).astype(jnp.float32) / 256.0
    own_resid = resid.astype(jnp.float32)
    outputs = jnp.dot(hidden, down_w, preferred_element_type=jnp.float32)
    mine = lax.psum_scatter(outputs, "hid", scatter_dimension=1, tiled=True)
    returned = lax.all_to_all(
        mine.reshape(sections, capacity, local_width),
        "sect",
        split_axis=0,
        concat_axis=0,
        tiled=True,
    )
    picked = returned.reshape(sections * capacity, local_width)[targets]
    mixture = jnp.sum((picked * weights[:, None]).reshape(tokens_here, 2, local_width), axis=1)
    new_local = (own_resid + mixture).astype(jnp.bfloat16)
    full_rows = lax.all_gather(new_local, "hid", axis=1, tiled=True)
    normed_next = layer_norm(full_rows.astype(jnp.float32), attn_gain)
    query = jnp.dot(
        normed_next,
        lax.all_gather(w_q, "sect", axis=0, tiled=True),
        preferred_element_type=jnp.float32,
    )
    keys = jnp.dot(
        normed_next,
        lax.all_gather(w_k, "sect", axis=0, tiled=True),
        preferred_element_type=jnp.float32,
    )
    vals = jnp.dot(
        normed_next,
        lax.all_gather(w_v, "sect", axis=0, tiled=True),
        preferred_element_type=jnp.float32,
    )
    context = attend(query, keys, vals.astype(jnp.bfloat16), doc_lengths[0], HD, H // KVH)
    return (new_local, context)


def solution(mesh):
    in_specs = (
        P(("groups", "sect"), "hid"),
        P(),
        P(("groups", "sect"), None),
        P(("groups", "sect"), None),
        P(("groups", "sect"), None),
        P("sect", None, "hid"),
        P("sect", None, "hid"),
        P("sect", "hid", None),
        P(),
        P("sect", "hid"),
        P("sect", "hid"),
        P("sect", "hid"),
    )
    out_specs = (P(("groups", "sect"), "hid"), P(("groups", "sect"), "hid"))
    plan = on_device
    if dict(mesh.shape) == {"groups": 2, "sect": 4, "hid": 4}:
        plan = on_grid
    return jax.shard_map(
        plan, mesh=mesh, in_specs=in_specs, out_specs=out_specs, check_vma=False
    )
```

```python
import math

import jax
import jax.numpy as jnp
from jax import lax
from jax.experimental import pallas as pl
from jax.experimental.pallas import tpu as pltpu
from jax.sharding import PartitionSpec as P

H = 32
KVH = 8
HD = 128
F32 = jnp.float32
BF16 = jnp.bfloat16
LIMIT = 16
SLOTS = 4
DEEP = 1024
ORDER = (3, 1, 2, 0)
TINY = pl.CostEstimate(flops=1, transcendentals=0, bytes_accessed=1)
STEP = pl.CostEstimate(flops=1 << 22, transcendentals=0, bytes_accessed=1 << 10)
VMEM = pl.BlockSpec(memory_space=pltpu.VMEM)
SMEM = pl.BlockSpec(memory_space=pltpu.SMEM)


def reads(count):
    return pl.CostEstimate(flops=1, transcendentals=0, bytes_accessed=count)


def features(piece):
    return pl.BlockSpec((piece.shape[0], piece.shape[1] // 1024 * 1024), lambda *_: (0, 0))


def routing(piece):
    return pl.BlockSpec((piece.shape[0], 128), lambda *_: (0, piece.shape[1] // 128 - 1))


def whole(shape):
    return pl.BlockSpec(shape, lambda *_: (0,) * len(shape))


def stats_body(before, first_ref, *refs):
    pieces = [first_ref] + list(refs[:-4]) if before else [first_ref] + list(refs[:-2])
    rows, local = first_ref.shape
    mean_ref, spread_ref = refs[-2], refs[-1]
    for j, p in enumerate(pieces):
        here = slice(j * rows, (j + 1) * rows)
        values = p[...].astype(F32)
        mean = jnp.sum(values, axis=1, keepdims=True) / local
        values = values - mean
        spread = jnp.sum(values * values, axis=1, keepdims=True)
        if before:
            seen = before * local
            old = refs[-4][here, :]
            gap = mean - old
            spread = refs[-3][here, :] + spread + gap * gap * (seen * local / (seen + local))
            mean = old + gap * (local / (seen + local))
        mean_ref[here, :] = mean
        spread_ref[here, :] = spread


def stats_call(pieces, seen, before, cost, name):
    rows = sum(p.shape[0] for p in pieces)
    operands = list(pieces) + list(before or ())
    return pl.pallas_call(
        lambda *refs: stats_body(seen, *refs),
        grid=(1,),
        in_specs=[features(v) for v in pieces] + [whole(v.shape) for v in before or ()],
        out_specs=[whole((rows, 1))] * 2,
        out_shape=[jax.ShapeDtypeStruct((rows, 1), F32)] * 2,
        compiler_params=pltpu.CompilerParams(vmem_limit_bytes=LIMIT << 20),
        cost_estimate=cost,
        name=name,
    )(*operands)


def stats_chain(groups, name):
    before = None
    for seen, pieces in enumerate(groups):
        before = list(stats_call(pieces, seen, before, STEP, name))
    return before


def full_norm_rows(pieces, gain_ref, hid, out_ref, first, step):
    rows, local = pieces[0].shape
    width = local * len(pieces)

    def body(i, carry):
        at = pl.multiple_of(i * step, step)
        values = [p[pl.ds(at, step), :].astype(F32) for p in pieces]
        total = values[0]
        for v in values[1:]:
            total = total + v
        mean = jnp.sum(total, axis=1, keepdims=True) / width
        centered = [v - mean for v in values]
        squares = centered[0] * centered[0]
        for c in centered[1:]:
            squares = squares + c * c
        spread = jnp.sum(squares, axis=1, keepdims=True) / width
        scale = lax.rsqrt(spread + 1e-05)
        for k, c in enumerate(centered):
            cols = pl.ds(pl.multiple_of((hid ^ k) * local, local), local)
            gain = gain_ref[:, cols].astype(F32)
            out_ref[pl.ds(first + at, step), cols] = (c * scale * gain).astype(BF16)
        return carry

    lax.fori_loop(0, rows // step, body, 0)


def norm_rows(pieces, gain_ref, mean_ref, spread_ref, hid, out_ref, first, step):
    rows, local = pieces[0].shape
    width = local * len(pieces)
    for k, p in enumerate(pieces):
        cols = pl.ds(pl.multiple_of((hid ^ k) * local, local), local)
        gain = gain_ref[:, cols].astype(F32)
        for at in range(0, rows, step):
            here = slice(first + at, first + at + step)
            scale = lax.rsqrt(spread_ref[here, :] / width + 1e-05)
            values = p[at : at + step, :].astype(F32) - mean_ref[here, :]
            out_ref[here, cols] = (values * scale * gain).astype(BF16)


def expert_body(place_ref, *refs):
    pieces = refs[:8]
    gain_ref, gate_hbm, up_hbm, down_hbm = refs[8:12]
    routed, keep_ref, send_ref = refs[12:14], refs[14], refs[15]
    normed, sums, hidden, ring, sems = refs[16:]
    rows, local = pieces[1].shape
    slots, deep = ring.shape[:2]
    width, units = gate_hbm.shape
    ups = 2 * (width // deep)
    hid, sect = place_ref[1], place_ref[2]

    def copy(n):
        if n < ups:
            src = (gate_hbm, up_hbm)[n % 2].at[n // 2 * deep : (n // 2 + 1) * deep, :]
        else:
            at = pl.multiple_of((hid ^ ORDER[n - ups]) * local, local)
            src = down_hbm.at[:, pl.ds(at, local)]
        return pltpu.make_async_copy(src, ring.at[n % slots], sems.at[n % slots])

    for n in range(slots):
        copy(n).start()
    for j in range(2):
        mine = pieces[4 * j : 4 * j + 4]
        full_norm_rows(mine, gain_ref, hid, normed, j * rows, 64)
    shares = []
    for ref in routed:
        chosen = lax.broadcasted_iota(jnp.int32, ref.shape, 1) == sect
        units_of = jnp.sum(jnp.where(chosen, ref[...].astype(F32), 0.0), axis=1, keepdims=True)
        shares.append(units_of / 256.0)
    for n in range(ups + 4):
        copy(n).wait()
        if n < ups:
            lhs = normed[:, n // 2 * deep : (n // 2 + 1) * deep]
            term = jnp.dot(lhs, ring[n % slots], preferred_element_type=F32)
            sums[n % 2] = term if n < 2 else sums[n % 2] + term
        else:
            if n == ups:
                for b in range(0, units, 128):
                    gate = sums[0, :, b : b + 128]
                    up = sums[1, :, b : b + 128]
                    hidden[:, b : b + 128] = (gate / (1.0 + jnp.exp(-gate)) * up).astype(BF16)
            out = jnp.dot(hidden[...], ring[n % slots], preferred_element_type=F32)
            keep_ref[n - ups] = out[:rows] * shares[0]
            send_ref[n - ups] = (out[rows:] * shares[1]).astype(BF16)
        if n + slots < ups + 4:
            copy(n + slots).start()


def expert_call(place, pieces, gain, gate_w, up_w, down_w, name):
    rows, local = pieces[1].shape
    width, units = gate_w.shape
    once = pl.Buffered(1)
    held = [pl.BlockSpec((rows, local), lambda *_: (0, 0), pipeline_mode=once)] * 8
    pieces = [pltpu.with_memory_space_constraint(p, pltpu.HBM) for p in pieces]
    routed = [pieces[0], pieces[4]]
    shape = (4, rows, local)
    return pl.pallas_call(
        expert_body,
        grid=(1,),
        in_specs=[SMEM]
        + held
        + [whole(gain.shape)]
        + [pl.BlockSpec(memory_space=pl.ANY)] * 3
        + [routing(v) for v in routed],
        out_specs=[whole(shape)] * 2,
        out_shape=[jax.ShapeDtypeStruct(shape, F32), jax.ShapeDtypeStruct(shape, BF16)],
        scratch_shapes=[
            pltpu.VMEM((2 * rows, width), BF16),
            pltpu.VMEM((2, 2 * rows, units), F32),
            pltpu.VMEM((2 * rows, units), BF16),
            pltpu.VMEM((SLOTS, DEEP, units), BF16),
            pltpu.SemaphoreType.DMA((SLOTS,)),
        ],
        compiler_params=pltpu.CompilerParams(vmem_limit_bytes=26 << 20),
        cost_estimate=TINY,
        name=name,
    )(place, *pieces, gain, gate_w, up_w, down_w, *routed)


def sums_call(body, operands, outs, name):
    specs = []
    for i, v in enumerate(operands):
        if isinstance(v, tuple):
            operands[i], n = v
            half = (v[0].shape[0] // 2,) + v[0].shape[1:]
            specs.append(pl.BlockSpec(half, lambda *_, n=n: (n, 0, 0)))
        else:
            specs.append(whole(v.shape))
    return pl.pallas_call(
        body,
        grid=(1,),
        in_specs=specs,
        out_specs=[whole(shape) for shape, _ in outs],
        out_shape=[jax.ShapeDtypeStruct(*o) for o in outs],
        compiler_params=pltpu.CompilerParams(vmem_limit_bytes=LIMIT << 20),
        cost_estimate=TINY,
        name=name,
    )(*operands)


def core_body(keep_ref, got_ref, first_ref, second_ref):
    for n in range(4):
        out_ref = (first_ref, second_ref)[n // 2]
        out_ref[n % 2] = (keep_ref[n] + got_ref[n].astype(F32)).astype(BF16)


def chip_body(keep_ref, near_ref, far_ref, out_ref):
    for n in range(2):
        total = keep_ref[n] + near_ref[n].astype(F32) + far_ref[n].astype(F32)
        out_ref[n] = total.astype(BF16)


def pair_body(keep_ref, near_ref, far_ref, hid_ref, resid_ref, send_ref, own_ref):
    both = []
    for n in range(2):
        total = keep_ref[n + 2] + near_ref[n + 2].astype(F32) + far_ref[n].astype(F32)
        both.append(total + hid_ref[n].astype(F32))
    send_ref[...] = both[0].astype(BF16)
    own_ref[...] = resid_ref[...].astype(F32) + both[1]


def last_body(own_ref, got_ref, out_ref):
    out_ref[...] = (own_ref[...] + got_ref[...].astype(F32)).astype(BF16)


def attend_body(place_ref, *refs):
    pieces = refs[:4]
    mean_ref, spread_ref, gain_ref, cos_ref, sin_ref, bias_ref = refs[4:10]
    sources = refs[10:24]
    out_ref, normed, total = refs[24:27]
    weights = refs[27:41]
    sems = refs[41]
    rows, local = pieces[0].shape
    half = local // 2
    group, hid, sect = place_ref[0], place_ref[1], place_ref[2]
    copies = [
        pltpu.make_async_copy(src, dst, sems.at[i])
        for i, (src, dst) in enumerate(zip(sources, weights))
    ]
    for c in copies:
        c.start()
    norm_rows(pieces, gain_ref, mean_ref, spread_ref, hid, normed, 0, 64)

    def rows_of(at, count):
        return normed[:, pl.ds(pl.multiple_of(at, 512), count)]

    starts = [(sect ^ j) * local for j in range(4)]
    mine, other = group * half, (1 - group) * half
    halves = [rows_of(starts[j] + o, half) for j in (2, 3) for o in (mine, other)]
    wholes = [rows_of(at, local) for at in starts]
    plan = []
    for c in range(2):
        cols = slice(c * half, (c + 1) * half)
        plan.append([(wholes[i], i, cols) for i in range(2)])
        plan[c] += [(halves[i], 2 + 4 * c + i, slice(0, half)) for i in range(4)]
    plan.append([(wholes[i], 10 + i, slice(0, half)) for i in range(4)])
    waited = set()
    for c, terms in enumerate(plan):
        acc = None
        for lhs, n, cols in terms:
            if n not in waited:
                copies[n].wait()
                waited.add(n)
            term = jnp.dot(lhs, weights[n][:, cols], preferred_element_type=F32)
            acc = term if acc is None else acc + term
        total[:, c * half : (c + 1) * half] = acc
    heads = local // HD
    kv_heads = (total.shape[1] - local) // (2 * HD)
    cos, sin, bias = cos_ref[...], sin_ref[...], bias_ref[...]

    def turned(at):
        x = total[:, at : at + HD]
        return (x * cos + pltpu.roll(x, HD // 2, 1) * sin).astype(BF16)

    for g in range(kv_heads):
        key = turned(local + g * HD)
        at = local + (kv_heads + g) * HD
        val = total[:, at : at + HD].astype(BF16)
        for r in range(heads // kv_heads):
            at = (g * (heads // kv_heads) + r) * HD
            scores = lax.dot_general(
                turned(at), key, (((1,), (1,)), ((), ())), preferred_element_type=F32
            ) * (1.0 / math.sqrt(HD)) + bias
            weight = jnp.exp(scores - jnp.max(scores, axis=1, keepdims=True))
            probs = (weight / jnp.sum(weight, axis=1, keepdims=True)).astype(BF16)
            mixed = jnp.dot(probs, val, preferred_element_type=F32)
            out_ref[:, at : at + HD] = mixed.astype(BF16)


def attend_call(place, pieces, stats, gain, cos, sin, bias, weights):
    rows, local = pieces[0].shape
    return pl.pallas_call(
        attend_body,
        grid=(1,),
        in_specs=[SMEM]
        + [whole(v.shape) for v in (*pieces, *stats, gain, cos, sin, bias)]
        + [pl.BlockSpec(memory_space=pl.ANY)] * len(weights),
        out_specs=whole((rows, local)),
        out_shape=jax.ShapeDtypeStruct((rows, local), BF16),
        scratch_shapes=[pltpu.VMEM((rows, 4 * local), BF16), pltpu.VMEM((rows, 3 * local // 2), F32)]
        + [pltpu.VMEM(w.shape, BF16) for w in weights]
        + [pltpu.SemaphoreType.DMA((len(weights),))],
        compiler_params=pltpu.CompilerParams(vmem_limit_bytes=20 << 20),
        cost_estimate=TINY,
        name="attend",
    )(place, *pieces, *stats, gain, cos, sin, bias, *weights)


def swap(value, axis, size, by):
    return lax.ppermute(value, axis, [(i, i ^ by) for i in range(size)])


def tie(*values):
    return lax.optimization_barrier(values)


def position_tables(lengths, count):
    ends = jnp.cumsum(lengths, dtype=jnp.int32)
    places = jnp.arange(count, dtype=jnp.int32)
    past = (places[:, None] >= ends[None, :]).astype(jnp.int32)
    doc_ids = jnp.sum(past, axis=1, dtype=jnp.int32)
    starts = jnp.sum(past * lengths[None, :], axis=1, dtype=jnp.int32)
    position = (places - starts).astype(F32)
    half = HD // 2
    freqs = jnp.exp(jnp.arange(half, dtype=F32) * (-2.0 * math.log(10000.0) / HD))
    angles = position[:, None] * freqs[None, :]
    cosine = jnp.cos(angles)
    sine = jnp.sin(angles)
    allowed = (doc_ids[:, None] == doc_ids[None, :]) & (places[None, :] <= places[:, None])
    bias = jnp.where(allowed, 0.0, -jnp.inf).astype(F32)
    return (
        jnp.concatenate([cosine, cosine], axis=1),
        jnp.concatenate([-sine, sine], axis=1),
        bias,
    )


def on_grid(
    resid, moe_gain, routes, gate_q, doc_lengths, w_gate, w_up, w_down, attn_gain, w_q, w_k, w_v
):
    tokens, local = resid.shape
    half = local // 2
    group = lax.axis_index("groups")
    sect = lax.axis_index("sect")
    hid = lax.axis_index("hid")
    place = jnp.stack([group, hid, sect]).astype(jnp.int32)

    over_hid = lambda v, by: swap(v, "hid", 4, by)
    over_core = lambda v: swap(v, "sect", 4, 1)
    over_chip = lambda v: swap(v, "sect", 4, 2)
    over_group = lambda v: swap(v, "groups", 2, 1)

    def half_of(w, c):
        return lax.dynamic_slice(w, (group * half, c * half), (half, half))

    here, there, here_core, there_core = ([None] * 2 for _ in range(4))
    gate_w, up_w, down_w = (
        pltpu.with_memory_space_constraint(w[0], pltpu.HBM) for w in (w_gate, w_up, w_down)
    )

    first, second = over_hid(resid, 1), over_hid(resid, 2)
    experts = jnp.arange(128, dtype=jnp.int32)
    units = jnp.sum(jnp.where(routes[:, :, None] == experts, gate_q[:, :, None], 0), axis=1)
    marked = jnp.concatenate([resid, units.astype(BF16)], axis=1)
    far_own = over_chip(marked)
    here[0] = over_chip(half_of(w_q, 0))
    w_kv = jnp.concatenate([w_k, w_v], axis=1)
    waiting = [half_of(w_q, 1)]
    tables = position_tables(doc_lengths[0], tokens)
    first, second, far_own, marked, w_q, w_kv, *held = tie(
        first, second, far_own, marked, w_q, w_kv, *waiting, *tables
    )
    waiting, tables = held[:1], held[1:]
    third = over_hid(second, 1)
    far = [far_own, over_chip(first), over_chip(second), None]
    near_pair = [over_core(marked), over_core(first), over_core(second), None]
    third, far[1], here[0] = tie(third, far[1], here[0])
    far[3], near_pair[3] = over_chip(third), over_core(third)
    near = [marked, first, second, third]
    far_pair = [over_core(far[0]), over_core(far[1]), None, None]

    gain = moe_gain.reshape(1, -1)
    weights = (gate_w, up_w, down_w)
    near_keep, near_send = expert_call(place, near + near_pair, gain, *weights, "near")
    near_send, far_pair[0], far_pair[1], *far = tie(near_send, far_pair[0], far_pair[1], *far)
    far_pair[2:] = [over_core(v) for v in far[2:]]
    far[3], waiting[0] = tie(far[3], waiting[0])
    here[1] = over_chip(waiting[0])
    far_keep, far_send = expert_call(place, far + far_pair, gain, *weights, "far")
    far_send, near_send, here[0], here[1] = tie(far_send, near_send, here[0], here[1])

    rows_of = (2, tokens, local)
    near_got, there[0] = over_core(near_send), over_group(here[0])
    operands = [far_keep, over_core(far_send)]
    summed = list(sums_call(core_body, operands, [(rows_of, BF16)] * 2, "sum_core"))
    got = over_chip(summed[0])
    got, near_got, there[0], here[0], here[1], summed[1] = tie(
        got, near_got, there[0], here[0], here[1], summed[1]
    )
    got_rest, there[1] = over_chip(summed[1]), over_group(here[1])
    here_core[0], there_core[0] = over_core(here[0]), over_core(there[0])
    operands = [near_keep, near_got, got]
    (part,) = sums_call(chip_body, operands, [(rows_of, BF16)], "sum_chip")
    part = over_hid(part, 1)
    part, got_rest, there[1], here_core[0], there_core[0], here[1], w_q, w_kv = tie(
        part, got_rest, there[1], here_core[0], there_core[0], here[1], w_q, w_kv
    )
    kv_far, q_near = over_chip(w_kv), over_core(w_q)
    here_core[1], there_core[1] = over_core(here[1]), over_core(there[1])
    operands = [near_keep, near_got, got_rest, part, resid]
    one = (tokens, local)
    send, own = sums_call(pair_body, operands, [(one, BF16), (one, F32)], "sum_pair")
    send = over_hid(send, 2)
    send, q_near, here_core[1], there_core[1], w_kv = tie(
        send, q_near, here_core[1], there_core[1], w_kv
    )
    (new_local,) = sums_call(last_body, [own, send], [(one, BF16)], "sum_hid")

    kv_near = over_core(w_kv)
    rows = [new_local, over_hid(new_local, 1), over_hid(new_local, 2), None]
    rows[1], rows[2], kv_near, kv_far = tie(rows[1], rows[2], kv_near, kv_far)
    rows[3] = over_hid(rows[2], 1)
    moved = [(here[c], there[c], here_core[c], there_core[c]) for c in range(2)]
    proj = [w_q, q_near, *moved[0], *moved[1], w_kv, kv_near, kv_far, over_core(kv_far)]
    stats = stats_chain([[r] for r in rows], "stats_next")
    gain = attn_gain.reshape(1, -1)
    context = attend_call(place, rows, stats, gain, *tables, proj)
    return (new_local, context)


def layer_norm(values, gain):
    center = values - jnp.mean(values, axis=1, keepdims=True)
    spread = jnp.mean(center * center, axis=1, keepdims=True)
    return (center * lax.rsqrt(spread + 1e-05) * gain.astype(jnp.float32)).astype(jnp.bfloat16)


def slot_targets(route_rows, experts, capacity):
    flat = route_rows.reshape(-1)
    onehot = (flat[:, None] == jnp.arange(experts, dtype=jnp.int32)[None, :]).astype(jnp.int32)
    before = jnp.cumsum(onehot, axis=0, dtype=jnp.int32) - onehot
    return flat * capacity + jnp.sum(before * onehot, axis=1, dtype=jnp.int32)


def source_rows(targets, experts, capacity):
    count = targets.shape[0]
    filler = jnp.full((experts * capacity,), count, jnp.int32)
    return filler.at[targets].set(jnp.arange(count, dtype=jnp.int32)) // 2


def rotate(values, position, head):
    count = values.shape[0]
    split_heads = values.reshape(count, -1, head)
    half = head // 2
    freqs = jnp.exp(jnp.arange(half, dtype=jnp.float32) * (-2.0 * math.log(10000.0) / head))
    angles = position[:, None, None] * freqs[None, None, :]
    cosine = jnp.cos(angles)
    sine = jnp.sin(angles)
    first = split_heads[:, :, :half]
    second = split_heads[:, :, half:]
    turned = jnp.concatenate(
        [first * cosine - second * sine, second * cosine + first * sine], axis=2
    )
    return turned.reshape(count, -1)


def attend(query, keys, vals, lengths, head, group):
    count = query.shape[0]
    kv_heads = keys.shape[1] // head
    ends = jnp.cumsum(lengths, dtype=jnp.int32)
    places = jnp.arange(count, dtype=jnp.int32)
    after = (places[:, None] >= ends[None, :]).astype(jnp.int32)
    doc_ids = jnp.sum(after, axis=1, dtype=jnp.int32)
    starts = jnp.sum(after * lengths[None, :], axis=1, dtype=jnp.int32)
    position = (places - starts).astype(jnp.float32)
    rotated_q = (
        rotate(query, position, head).astype(jnp.bfloat16).reshape(count, kv_heads, group, head)
    )
    rotated_k = rotate(keys, position, head).astype(jnp.bfloat16).reshape(count, kv_heads, head)
    value_heads = vals.reshape(count, kv_heads, head)
    allowed = (doc_ids[:, None] == doc_ids[None, :]) & (places[None, :] <= places[:, None])
    scores = jnp.einsum(
        "tkgd,skd->kgts", rotated_q, rotated_k, preferred_element_type=jnp.float32
    ) * (1.0 / math.sqrt(head))
    scores = jnp.where(allowed[None, None], scores, -jnp.inf)
    highest = jnp.max(scores, axis=3, keepdims=True)
    weights = jnp.exp(scores - highest)
    probs = (weights / jnp.sum(weights, axis=3, keepdims=True)).astype(jnp.bfloat16)
    mixed = jnp.einsum("kgts,skd->tkgd", probs, value_heads, preferred_element_type=jnp.float32)
    return mixed.astype(jnp.bfloat16).reshape(count, -1)


def on_device(
    resid, moe_gain, routes, gate_q, doc_lengths, w_gate, w_up, w_down, attn_gain, w_q, w_k, w_v
):
    sections = lax.axis_size("sect")
    slices = lax.axis_size("hid")
    tokens_here, local_width = resid.shape
    width = local_width * slices
    capacity = 4 * tokens_here // sections
    entry = lax.all_gather(resid, "hid", axis=1, tiled=True)
    normed = layer_norm(entry.astype(jnp.float32), moe_gain)
    targets = slot_targets(routes, sections, capacity)
    sources = source_rows(targets, sections, capacity)
    padded = jnp.concatenate([normed, jnp.zeros((1, width), jnp.bfloat16)], axis=0)
    gate_w = w_gate[0]
    up_w = w_up[0]
    down_w = w_down[0]
    outgoing = padded[sources].reshape(sections, capacity, width)
    arrived = lax.all_to_all(outgoing, "sect", split_axis=0, concat_axis=0, tiled=True).reshape(
        sections * capacity, width
    )
    gate = jnp.dot(arrived, gate_w, preferred_element_type=jnp.float32)
    up = jnp.dot(arrived, up_w, preferred_element_type=jnp.float32)
    hidden = (jax.nn.silu(gate) * up).astype(jnp.bfloat16)
    weights = gate_q.reshape(-1).astype(jnp.float32) / 256.0
    own_resid = resid.astype(jnp.float32)
    outputs = jnp.dot(hidden, down_w, preferred_element_type=jnp.float32)
    mine = lax.psum_scatter(outputs, "hid", scatter_dimension=1, tiled=True)
    returned = lax.all_to_all(
        mine.reshape(sections, capacity, local_width),
        "sect",
        split_axis=0,
        concat_axis=0,
        tiled=True,
    )
    picked = returned.reshape(sections * capacity, local_width)[targets]
    mixture = jnp.sum((picked * weights[:, None]).reshape(tokens_here, 2, local_width), axis=1)
    new_local = (own_resid + mixture).astype(jnp.bfloat16)
    full_rows = lax.all_gather(new_local, "hid", axis=1, tiled=True)
    normed_next = layer_norm(full_rows.astype(jnp.float32), attn_gain)
    query = jnp.dot(
        normed_next,
        lax.all_gather(w_q, "sect", axis=0, tiled=True),
        preferred_element_type=jnp.float32,
    )
    keys = jnp.dot(
        normed_next,
        lax.all_gather(w_k, "sect", axis=0, tiled=True),
        preferred_element_type=jnp.float32,
    )
    vals = jnp.dot(
        normed_next,
        lax.all_gather(w_v, "sect", axis=0, tiled=True),
        preferred_element_type=jnp.float32,
    )
    context = attend(query, keys, vals.astype(jnp.bfloat16), doc_lengths[0], HD, H // KVH)
    return (new_local, context)


def solution(mesh):
    in_specs = (
        P(("groups", "sect"), "hid"),
        P(),
        P(("groups", "sect"), None),
        P(("groups", "sect"), None),
        P(("groups", "sect"), None),
        P("sect", None, "hid"),
        P("sect", None, "hid"),
        P("sect", "hid", None),
        P(),
        P("sect", "hid"),
        P("sect", "hid"),
        P("sect", "hid"),
    )
    out_specs = (P(("groups", "sect"), "hid"), P(("groups", "sect"), "hid"))
    plan = on_device
    if dict(mesh.shape) == {"groups": 2, "sect": 4, "hid": 4}:
        plan = on_grid
    return jax.shard_map(
        plan, mesh=mesh, in_specs=in_specs, out_specs=out_specs, check_vma=False
    )
```

```python
import math

import jax
import jax.numpy as jnp
from jax import lax
from jax.experimental import pallas as pl
from jax.experimental.pallas import tpu as pltpu
from jax.sharding import PartitionSpec as P

H = 32
KVH = 8
HD = 128
F32 = jnp.float32
BF16 = jnp.bfloat16
LIMIT = 16
SLOTS = 4
DEEP = 1024
ORDER = (3, 1, 2, 0)
TINY = pl.CostEstimate(flops=1, transcendentals=0, bytes_accessed=1)
STEP = pl.CostEstimate(flops=1 << 22, transcendentals=0, bytes_accessed=1 << 10)
VMEM = pl.BlockSpec(memory_space=pltpu.VMEM)
SMEM = pl.BlockSpec(memory_space=pltpu.SMEM)


def reads(count):
    return pl.CostEstimate(flops=1, transcendentals=0, bytes_accessed=count)


def features(piece):
    return pl.BlockSpec((piece.shape[0], piece.shape[1] // 1024 * 1024), lambda *_: (0, 0))


def routing(piece):
    return pl.BlockSpec((piece.shape[0], 128), lambda *_: (0, piece.shape[1] // 128 - 1))


def whole(shape):
    return pl.BlockSpec(shape, lambda *_: (0,) * len(shape))


def stats_body(before, first_ref, *refs):
    pieces = [first_ref] + list(refs[:-4]) if before else [first_ref] + list(refs[:-2])
    rows, local = first_ref.shape
    mean_ref, spread_ref = refs[-2], refs[-1]
    for j, p in enumerate(pieces):
        here = slice(j * rows, (j + 1) * rows)
        values = p[...].astype(F32)
        mean = jnp.sum(values, axis=1, keepdims=True) / local
        values = values - mean
        spread = jnp.sum(values * values, axis=1, keepdims=True)
        if before:
            seen = before * local
            old = refs[-4][here, :]
            gap = mean - old
            spread = refs[-3][here, :] + spread + gap * gap * (seen * local / (seen + local))
            mean = old + gap * (local / (seen + local))
        mean_ref[here, :] = mean
        spread_ref[here, :] = spread


def stats_call(pieces, seen, before, cost, name):
    rows = sum(p.shape[0] for p in pieces)
    operands = list(pieces) + list(before or ())
    return pl.pallas_call(
        lambda *refs: stats_body(seen, *refs),
        grid=(1,),
        in_specs=[features(v) for v in pieces] + [whole(v.shape) for v in before or ()],
        out_specs=[whole((rows, 1))] * 2,
        out_shape=[jax.ShapeDtypeStruct((rows, 1), F32)] * 2,
        compiler_params=pltpu.CompilerParams(vmem_limit_bytes=LIMIT << 20),
        cost_estimate=cost,
        name=name,
    )(*operands)


def stats_chain(groups, name):
    before = None
    for seen, pieces in enumerate(groups):
        before = list(stats_call(pieces, seen, before, STEP, name))
    return before


def full_norm_rows(pieces, gain_ref, hid, out_ref, first, step):
    rows, local = pieces[0].shape
    width = local * len(pieces)

    def body(i, carry):
        at = pl.multiple_of(i * step, step)
        values = [p[pl.ds(at, step), :].astype(F32) for p in pieces]
        total = values[0]
        for v in values[1:]:
            total = total + v
        mean = jnp.sum(total, axis=1, keepdims=True) / width
        centered = [v - mean for v in values]
        squares = centered[0] * centered[0]
        for c in centered[1:]:
            squares = squares + c * c
        spread = jnp.sum(squares, axis=1, keepdims=True) / width
        scale = lax.rsqrt(spread + 1e-05)
        for k, c in enumerate(centered):
            cols = pl.ds(pl.multiple_of((hid ^ k) * local, local), local)
            gain = gain_ref[:, cols].astype(F32)
            out_ref[pl.ds(first + at, step), cols] = (c * scale * gain).astype(BF16)
        return carry

    lax.fori_loop(0, rows // step, body, 0)


def norm_rows(pieces, gain_ref, mean_ref, spread_ref, hid, out_ref, first, step):
    rows, local = pieces[0].shape
    width = local * len(pieces)
    for k, p in enumerate(pieces):
        cols = pl.ds(pl.multiple_of((hid ^ k) * local, local), local)
        gain = gain_ref[:, cols].astype(F32)
        for at in range(0, rows, step):
            here = slice(first + at, first + at + step)
            scale = lax.rsqrt(spread_ref[here, :] / width + 1e-05)
            values = p[at : at + step, :].astype(F32) - mean_ref[here, :]
            out_ref[here, cols] = (values * scale * gain).astype(BF16)


def expert_body(place_ref, *refs):
    pieces = refs[:8]
    gain_ref, gate_hbm, up_hbm, down_hbm = refs[8:12]
    routed, keep_ref, send_ref = refs[12:14], refs[14], refs[15]
    normed, sums, hidden, ring, sems = refs[16:]
    rows, local = pieces[1].shape
    slots, deep = ring.shape[:2]
    width, units = gate_hbm.shape
    ups = 2 * (width // deep)
    hid, sect = place_ref[1], place_ref[2]

    def copy(n):
        if n < ups:
            src = (gate_hbm, up_hbm)[n % 2].at[n // 2 * deep : (n // 2 + 1) * deep, :]
        else:
            at = pl.multiple_of((hid ^ ORDER[n - ups]) * local, local)
            src = down_hbm.at[:, pl.ds(at, local)]
        return pltpu.make_async_copy(src, ring.at[n % slots], sems.at[n % slots])

    for n in range(slots):
        copy(n).start()
    for j in range(2):
        mine = pieces[4 * j : 4 * j + 4]
        full_norm_rows(mine, gain_ref, hid, normed, j * rows, 64)
    shares = []
    for ref in routed:
        chosen = lax.broadcasted_iota(jnp.int32, ref.shape, 1) == sect
        units_of = jnp.sum(jnp.where(chosen, ref[...].astype(F32), 0.0), axis=1, keepdims=True)
        shares.append(units_of / 256.0)
    for n in range(ups + 4):
        copy(n).wait()
        if n < ups:
            lhs = normed[:, n // 2 * deep : (n // 2 + 1) * deep]
            term = jnp.dot(lhs, ring[n % slots], preferred_element_type=F32)
            sums[n % 2] = term if n < 2 else sums[n % 2] + term
        else:
            if n == ups:
                for b in range(0, units, 128):
                    gate = sums[0, :, b : b + 128]
                    up = sums[1, :, b : b + 128]
                    hidden[:, b : b + 128] = (gate / (1.0 + jnp.exp(-gate)) * up).astype(BF16)
            out = jnp.dot(hidden[...], ring[n % slots], preferred_element_type=F32)
            keep_ref[n - ups] = out[:rows] * shares[0]
            send_ref[n - ups] = (out[rows:] * shares[1]).astype(BF16)
        if n + slots < ups + 4:
            copy(n + slots).start()


def expert_call(place, pieces, gain, gate_w, up_w, down_w, name):
    rows, local = pieces[1].shape
    width, units = gate_w.shape
    once = pl.Buffered(1)
    held = [pl.BlockSpec((rows, local), lambda *_: (0, 0), pipeline_mode=once)] * 8
    fixed = [pltpu.with_memory_space_constraint(p, pltpu.HBM) for p in pieces[:4]]
    pieces = fixed + list(pieces[4:])
    routed = [pieces[0], pieces[4]]
    shape = (4, rows, local)
    return pl.pallas_call(
        expert_body,
        grid=(1,),
        in_specs=[SMEM]
        + held
        + [whole(gain.shape)]
        + [pl.BlockSpec(memory_space=pl.ANY)] * 3
        + [routing(v) for v in routed],
        out_specs=[whole(shape)] * 2,
        out_shape=[jax.ShapeDtypeStruct(shape, F32), jax.ShapeDtypeStruct(shape, BF16)],
        scratch_shapes=[
            pltpu.VMEM((2 * rows, width), BF16),
            pltpu.VMEM((2, 2 * rows, units), F32),
            pltpu.VMEM((2 * rows, units), BF16),
            pltpu.VMEM((SLOTS, DEEP, units), BF16),
            pltpu.SemaphoreType.DMA((SLOTS,)),
        ],
        compiler_params=pltpu.CompilerParams(vmem_limit_bytes=26 << 20),
        cost_estimate=TINY,
        name=name,
    )(place, *pieces, gain, gate_w, up_w, down_w, *routed)


def sums_call(body, operands, outs, name):
    specs = []
    for i, v in enumerate(operands):
        if isinstance(v, tuple):
            operands[i], n = v
            half = (v[0].shape[0] // 2,) + v[0].shape[1:]
            specs.append(pl.BlockSpec(half, lambda *_, n=n: (n, 0, 0)))
        else:
            specs.append(whole(v.shape))
    return pl.pallas_call(
        body,
        grid=(1,),
        in_specs=specs,
        out_specs=[whole(shape) for shape, _ in outs],
        out_shape=[jax.ShapeDtypeStruct(*o) for o in outs],
        compiler_params=pltpu.CompilerParams(vmem_limit_bytes=LIMIT << 20),
        cost_estimate=TINY,
        name=name,
    )(*operands)


def core_body(keep_ref, got_ref, first_ref, second_ref):
    for n in range(4):
        out_ref = (first_ref, second_ref)[n // 2]
        out_ref[n % 2] = (keep_ref[n] + got_ref[n].astype(F32)).astype(BF16)


def chip_body(keep_ref, near_ref, far_ref, out_ref):
    for n in range(2):
        total = keep_ref[n] + near_ref[n].astype(F32) + far_ref[n].astype(F32)
        out_ref[n] = total.astype(BF16)


def pair_body(keep_ref, near_ref, far_ref, hid_ref, resid_ref, send_ref, own_ref):
    both = []
    for n in range(2):
        total = keep_ref[n + 2] + near_ref[n + 2].astype(F32) + far_ref[n].astype(F32)
        both.append(total + hid_ref[n].astype(F32))
    send_ref[...] = both[0].astype(BF16)
    own_ref[...] = resid_ref[...].astype(F32) + both[1]


def last_body(own_ref, got_ref, out_ref):
    out_ref[...] = (own_ref[...] + got_ref[...].astype(F32)).astype(BF16)


def stage_body(*refs):
    count = (len(refs) - 2) // 2
    copies = [
        pltpu.make_async_copy(refs[i], refs[count + i], refs[-1].at[i]) for i in range(count)
    ]
    for c in copies:
        c.start()
    refs[-2][...] = jnp.zeros_like(refs[-2])
    for c in copies:
        c.wait()


def stage_call(arrays, name):
    return pl.pallas_call(
        stage_body,
        in_specs=[pl.BlockSpec(memory_space=pl.ANY)] * len(arrays),
        out_specs=[VMEM] * (len(arrays) + 1),
        out_shape=[pltpu.VMEM(a.shape, a.dtype) for a in arrays]
        + [jax.ShapeDtypeStruct((8, 128), F32)],
        scratch_shapes=[pltpu.SemaphoreType.DMA((len(arrays),))],
        compiler_params=pltpu.CompilerParams(vmem_limit_bytes=LIMIT << 20),
        cost_estimate=TINY,
        name=name,
    )(*arrays)


def attend_body(place_ref, *refs):
    pieces = refs[:4]
    mean_ref, spread_ref, gain_ref, cos_ref, sin_ref, bias_ref = refs[4:10]
    weights = list(refs[10:23])
    last_hbm, out_ref, normed, total, last_ref, sem = refs[24:30]
    weights.append(last_ref)
    rows, local = pieces[0].shape
    half = local // 2
    group, hid, sect = place_ref[0], place_ref[1], place_ref[2]
    copy = pltpu.make_async_copy(last_hbm, last_ref, sem.at[0])
    copy.start()
    norm_rows(pieces, gain_ref, mean_ref, spread_ref, hid, normed, 0, 64)

    def rows_of(at, count):
        return normed[:, pl.ds(pl.multiple_of(at, 512), count)]

    starts = [(sect ^ j) * local for j in range(4)]
    mine, other = group * half, (1 - group) * half
    halves = [rows_of(starts[j] + o, half) for j in (2, 3) for o in (mine, other)]
    wholes = [rows_of(at, local) for at in starts]
    plan = []
    for c in range(2):
        cols = slice(c * half, (c + 1) * half)
        plan.append([(wholes[i], i, cols) for i in range(2)])
        plan[c] += [(halves[i], 2 + 4 * c + i, slice(0, half)) for i in range(4)]
    plan.append([(wholes[i], 10 + i, slice(0, half)) for i in range(4)])
    for c, terms in enumerate(plan):
        acc = None
        for lhs, n, cols in terms:
            if n == 13:
                copy.wait()
            term = jnp.dot(lhs, weights[n][:, cols], preferred_element_type=F32)
            acc = term if acc is None else acc + term
        total[:, c * half : (c + 1) * half] = acc
    heads = local // HD
    kv_heads = (total.shape[1] - local) // (2 * HD)
    cos, sin, bias = cos_ref[...], sin_ref[...], bias_ref[...]

    def turned(at):
        x = total[:, at : at + HD]
        return (x * cos + pltpu.roll(x, HD // 2, 1) * sin).astype(BF16)

    for g in range(kv_heads):
        key = turned(local + g * HD)
        at = local + (kv_heads + g) * HD
        val = total[:, at : at + HD].astype(BF16)
        for r in range(heads // kv_heads):
            at = (g * (heads // kv_heads) + r) * HD
            scores = lax.dot_general(
                turned(at), key, (((1,), (1,)), ((), ())), preferred_element_type=F32
            ) * (1.0 / math.sqrt(HD)) + bias
            weight = jnp.exp(scores - jnp.max(scores, axis=1, keepdims=True))
            probs = (weight / jnp.sum(weight, axis=1, keepdims=True)).astype(BF16)
            mixed = jnp.dot(probs, val, preferred_element_type=F32)
            out_ref[:, at : at + HD] = mixed.astype(BF16)


def attend_call(place, pieces, stats, gain, cos, sin, bias, weights):
    rows, local = pieces[0].shape
    return pl.pallas_call(
        attend_body,
        grid=(1,),
        in_specs=[SMEM]
        + [whole(v.shape) for v in (*pieces, *stats, gain, cos, sin, bias)]
        + [VMEM] * (len(weights) - 2)
        + [whole((8, 128)), pl.BlockSpec(memory_space=pl.ANY)],
        out_specs=whole((rows, local)),
        out_shape=jax.ShapeDtypeStruct((rows, local), BF16),
        scratch_shapes=[pltpu.VMEM((rows, 4 * local), BF16), pltpu.VMEM((rows, 3 * local // 2), F32)]
        + [pltpu.VMEM(weights[-1].shape, BF16)]
        + [pltpu.SemaphoreType.DMA((1,))],
        compiler_params=pltpu.CompilerParams(vmem_limit_bytes=20 << 20),
        cost_estimate=TINY,
        name="attend",
    )(place, *pieces, *stats, gain, cos, sin, bias, *weights)


def swap(value, axis, size, by):
    return lax.ppermute(value, axis, [(i, i ^ by) for i in range(size)])


def tie(*values):
    return lax.optimization_barrier(values)


def position_tables(lengths, count):
    ends = jnp.cumsum(lengths, dtype=jnp.int32)
    places = jnp.arange(count, dtype=jnp.int32)
    past = (places[:, None] >= ends[None, :]).astype(jnp.int32)
    doc_ids = jnp.sum(past, axis=1, dtype=jnp.int32)
    starts = jnp.sum(past * lengths[None, :], axis=1, dtype=jnp.int32)
    position = (places - starts).astype(F32)
    half = HD // 2
    freqs = jnp.exp(jnp.arange(half, dtype=F32) * (-2.0 * math.log(10000.0) / HD))
    angles = position[:, None] * freqs[None, :]
    cosine = jnp.cos(angles)
    sine = jnp.sin(angles)
    allowed = (doc_ids[:, None] == doc_ids[None, :]) & (places[None, :] <= places[:, None])
    bias = jnp.where(allowed, 0.0, -jnp.inf).astype(F32)
    return (
        jnp.concatenate([cosine, cosine], axis=1),
        jnp.concatenate([-sine, sine], axis=1),
        bias,
    )


def on_grid(
    resid, moe_gain, routes, gate_q, doc_lengths, w_gate, w_up, w_down, attn_gain, w_q, w_k, w_v
):
    tokens, local = resid.shape
    half = local // 2
    group = lax.axis_index("groups")
    sect = lax.axis_index("sect")
    hid = lax.axis_index("hid")
    place = jnp.stack([group, hid, sect]).astype(jnp.int32)

    over_hid = lambda v, by: swap(v, "hid", 4, by)
    over_core = lambda v: swap(v, "sect", 4, 1)
    over_chip = lambda v: swap(v, "sect", 4, 2)
    over_group = lambda v: swap(v, "groups", 2, 1)

    def half_of(w, c):
        return lax.dynamic_slice(w, (group * half, c * half), (half, half))

    here, there, here_core, there_core = ([None] * 2 for _ in range(4))
    gate_w, up_w, down_w = (
        pltpu.with_memory_space_constraint(w[0], pltpu.HBM) for w in (w_gate, w_up, w_down)
    )

    first, second = over_hid(resid, 1), over_hid(resid, 2)
    experts = jnp.arange(128, dtype=jnp.int32)
    units = jnp.sum(jnp.where(routes[:, :, None] == experts, gate_q[:, :, None], 0), axis=1)
    marked = jnp.concatenate([resid, units.astype(BF16)], axis=1)
    far_own = over_chip(marked)
    here[0] = over_chip(half_of(w_q, 0))
    w_kv = jnp.concatenate([w_k, w_v], axis=1)
    waiting = [half_of(w_q, 1)]
    tables = position_tables(doc_lengths[0], tokens)
    first, second, far_own, marked, w_q, w_kv, *held = tie(
        first, second, far_own, marked, w_q, w_kv, *waiting, *tables
    )
    waiting, tables = held[:1], held[1:]
    third = over_hid(second, 1)
    far = [far_own, over_chip(first), over_chip(second), None]
    near_pair = [over_core(marked), over_core(first), over_core(second), None]
    third, far[1], here[0] = tie(third, far[1], here[0])
    far[3], near_pair[3] = over_chip(third), over_core(third)
    near = [marked, first, second, third]
    far_pair = [over_core(far[0]), over_core(far[1]), None, None]

    gain = moe_gain.reshape(1, -1)
    weights = (gate_w, up_w, down_w)
    near_keep, near_send = expert_call(place, near + near_pair, gain, *weights, "near")
    near_send, far_pair[0], far_pair[1], *far = tie(near_send, far_pair[0], far_pair[1], *far)
    far_pair[2:] = [over_core(v) for v in far[2:]]
    far[3], waiting[0] = tie(far[3], waiting[0])
    here[1] = over_chip(waiting[0])
    far_keep, far_send = expert_call(place, far + far_pair, gain, *weights, "far")
    far_send, near_send, here[0], here[1] = tie(far_send, near_send, here[0], here[1])

    rows_of = (2, tokens, local)
    near_got, there[0] = over_core(near_send), over_group(here[0])
    operands = [far_keep, over_core(far_send)]
    summed = list(sums_call(core_body, operands, [(rows_of, BF16)] * 2, "sum_core"))
    got = over_chip(summed[0])
    got, near_got, there[0], here[0], here[1], summed[1] = tie(
        got, near_got, there[0], here[0], here[1], summed[1]
    )
    got_rest, there[1] = over_chip(summed[1]), over_group(here[1])
    here_core[0], there_core[0] = over_core(here[0]), over_core(there[0])
    operands = [near_keep, near_got, got]
    (part,) = sums_call(chip_body, operands, [(rows_of, BF16)], "sum_chip")
    part = over_hid(part, 1)
    part, got_rest, there[1], here_core[0], there_core[0], here[1], w_q, w_kv = tie(
        part, got_rest, there[1], here_core[0], there_core[0], here[1], w_q, w_kv
    )
    kv_far, q_near = over_chip(w_kv), over_core(w_q)
    here_core[1], there_core[1] = over_core(here[1]), over_core(there[1])
    operands = [near_keep, near_got, got_rest, part, resid]
    one = (tokens, local)
    send, own = sums_call(pair_body, operands, [(one, BF16), (one, F32)], "sum_pair")
    send = over_hid(send, 2)
    send, q_near, here_core[1], there_core[1], w_kv = tie(
        send, q_near, here_core[1], there_core[1], w_kv
    )
    (new_local,) = sums_call(last_body, [own, send], [(one, BF16)], "sum_hid")

    kv_near = over_core(w_kv)
    rows = [new_local, over_hid(new_local, 1), over_hid(new_local, 2), None]
    rows[1], rows[2], kv_near, kv_far = tie(rows[1], rows[2], kv_near, kv_far)
    rows[3] = over_hid(rows[2], 1)
    moved = [(here[c], there[c], here_core[c], there_core[c]) for c in range(2)]
    proj = [w_q, q_near, *moved[0], *moved[1], w_kv, kv_near, kv_far]
    *proj, token = stage_call(proj, "stage")
    rows[3], token = tie(rows[3], token)
    proj += [token, over_core(kv_far)]
    stats = stats_chain([[r] for r in rows], "stats_next")
    gain = attn_gain.reshape(1, -1)
    context = attend_call(place, rows, stats, gain, *tables, proj)
    return (new_local, context)


def layer_norm(values, gain):
    center = values - jnp.mean(values, axis=1, keepdims=True)
    spread = jnp.mean(center * center, axis=1, keepdims=True)
    return (center * lax.rsqrt(spread + 1e-05) * gain.astype(jnp.float32)).astype(jnp.bfloat16)


def slot_targets(route_rows, experts, capacity):
    flat = route_rows.reshape(-1)
    onehot = (flat[:, None] == jnp.arange(experts, dtype=jnp.int32)[None, :]).astype(jnp.int32)
    before = jnp.cumsum(onehot, axis=0, dtype=jnp.int32) - onehot
    return flat * capacity + jnp.sum(before * onehot, axis=1, dtype=jnp.int32)


def source_rows(targets, experts, capacity):
    count = targets.shape[0]
    filler = jnp.full((experts * capacity,), count, jnp.int32)
    return filler.at[targets].set(jnp.arange(count, dtype=jnp.int32)) // 2


def rotate(values, position, head):
    count = values.shape[0]
    split_heads = values.reshape(count, -1, head)
    half = head // 2
    freqs = jnp.exp(jnp.arange(half, dtype=jnp.float32) * (-2.0 * math.log(10000.0) / head))
    angles = position[:, None, None] * freqs[None, None, :]
    cosine = jnp.cos(angles)
    sine = jnp.sin(angles)
    first = split_heads[:, :, :half]
    second = split_heads[:, :, half:]
    turned = jnp.concatenate(
        [first * cosine - second * sine, second * cosine + first * sine], axis=2
    )
    return turned.reshape(count, -1)


def attend(query, keys, vals, lengths, head, group):
    count = query.shape[0]
    kv_heads = keys.shape[1] // head
    ends = jnp.cumsum(lengths, dtype=jnp.int32)
    places = jnp.arange(count, dtype=jnp.int32)
    after = (places[:, None] >= ends[None, :]).astype(jnp.int32)
    doc_ids = jnp.sum(after, axis=1, dtype=jnp.int32)
    starts = jnp.sum(after * lengths[None, :], axis=1, dtype=jnp.int32)
    position = (places - starts).astype(jnp.float32)
    rotated_q = (
        rotate(query, position, head).astype(jnp.bfloat16).reshape(count, kv_heads, group, head)
    )
    rotated_k = rotate(keys, position, head).astype(jnp.bfloat16).reshape(count, kv_heads, head)
    value_heads = vals.reshape(count, kv_heads, head)
    allowed = (doc_ids[:, None] == doc_ids[None, :]) & (places[None, :] <= places[:, None])
    scores = jnp.einsum(
        "tkgd,skd->kgts", rotated_q, rotated_k, preferred_element_type=jnp.float32
    ) * (1.0 / math.sqrt(head))
    scores = jnp.where(allowed[None, None], scores, -jnp.inf)
    highest = jnp.max(scores, axis=3, keepdims=True)
    weights = jnp.exp(scores - highest)
    probs = (weights / jnp.sum(weights, axis=3, keepdims=True)).astype(jnp.bfloat16)
    mixed = jnp.einsum("kgts,skd->tkgd", probs, value_heads, preferred_element_type=jnp.float32)
    return mixed.astype(jnp.bfloat16).reshape(count, -1)


def on_device(
    resid, moe_gain, routes, gate_q, doc_lengths, w_gate, w_up, w_down, attn_gain, w_q, w_k, w_v
):
    sections = lax.axis_size("sect")
    slices = lax.axis_size("hid")
    tokens_here, local_width = resid.shape
    width = local_width * slices
    capacity = 4 * tokens_here // sections
    entry = lax.all_gather(resid, "hid", axis=1, tiled=True)
    normed = layer_norm(entry.astype(jnp.float32), moe_gain)
    targets = slot_targets(routes, sections, capacity)
    sources = source_rows(targets, sections, capacity)
    padded = jnp.concatenate([normed, jnp.zeros((1, width), jnp.bfloat16)], axis=0)
    gate_w = w_gate[0]
    up_w = w_up[0]
    down_w = w_down[0]
    outgoing = padded[sources].reshape(sections, capacity, width)
    arrived = lax.all_to_all(outgoing, "sect", split_axis=0, concat_axis=0, tiled=True).reshape(
        sections * capacity, width
    )
    gate = jnp.dot(arrived, gate_w, preferred_element_type=jnp.float32)
    up = jnp.dot(arrived, up_w, preferred_element_type=jnp.float32)
    hidden = (jax.nn.silu(gate) * up).astype(jnp.bfloat16)
    weights = gate_q.reshape(-1).astype(jnp.float32) / 256.0
    own_resid = resid.astype(jnp.float32)
    outputs = jnp.dot(hidden, down_w, preferred_element_type=jnp.float32)
    mine = lax.psum_scatter(outputs, "hid", scatter_dimension=1, tiled=True)
    returned = lax.all_to_all(
        mine.reshape(sections, capacity, local_width),
        "sect",
        split_axis=0,
        concat_axis=0,
        tiled=True,
    )
    picked = returned.reshape(sections * capacity, local_width)[targets]
    mixture = jnp.sum((picked * weights[:, None]).reshape(tokens_here, 2, local_width), axis=1)
    new_local = (own_resid + mixture).astype(jnp.bfloat16)
    full_rows = lax.all_gather(new_local, "hid", axis=1, tiled=True)
    normed_next = layer_norm(full_rows.astype(jnp.float32), attn_gain)
    query = jnp.dot(
        normed_next,
        lax.all_gather(w_q, "sect", axis=0, tiled=True),
        preferred_element_type=jnp.float32,
    )
    keys = jnp.dot(
        normed_next,
        lax.all_gather(w_k, "sect", axis=0, tiled=True),
        preferred_element_type=jnp.float32,
    )
    vals = jnp.dot(
        normed_next,
        lax.all_gather(w_v, "sect", axis=0, tiled=True),
        preferred_element_type=jnp.float32,
    )
    context = attend(query, keys, vals.astype(jnp.bfloat16), doc_lengths[0], HD, H // KVH)
    return (new_local, context)


def solution(mesh):
    in_specs = (
        P(("groups", "sect"), "hid"),
        P(),
        P(("groups", "sect"), None),
        P(("groups", "sect"), None),
        P(("groups", "sect"), None),
        P("sect", None, "hid"),
        P("sect", None, "hid"),
        P("sect", "hid", None),
        P(),
        P("sect", "hid"),
        P("sect", "hid"),
        P("sect", "hid"),
    )
    out_specs = (P(("groups", "sect"), "hid"), P(("groups", "sect"), "hid"))
    plan = on_device
    if dict(mesh.shape) == {"groups": 2, "sect": 4, "hid": 4}:
        plan = on_grid
    return jax.shard_map(
        plan, mesh=mesh, in_specs=in_specs, out_specs=out_specs, check_vma=False
    )
```

```python
import math

import jax
import jax.numpy as jnp
from jax import lax
from jax.experimental import pallas as pl
from jax.experimental.pallas import tpu as pltpu
from jax.sharding import PartitionSpec as P

H = 32
KVH = 8
HD = 128
F32 = jnp.float32
BF16 = jnp.bfloat16
LIMIT = 16
SLOTS = 4
DEEP = 1024
ORDER = (3, 1, 2, 0)
TINY = pl.CostEstimate(flops=1, transcendentals=0, bytes_accessed=1)
STEP = pl.CostEstimate(flops=1 << 22, transcendentals=0, bytes_accessed=1 << 10)
VMEM = pl.BlockSpec(memory_space=pltpu.VMEM)
SMEM = pl.BlockSpec(memory_space=pltpu.SMEM)


def reads(count):
    return pl.CostEstimate(flops=1, transcendentals=0, bytes_accessed=count)


def features(piece):
    return pl.BlockSpec((piece.shape[0], piece.shape[1] // 1024 * 1024), lambda *_: (0, 0))


def routing(piece):
    return pl.BlockSpec((piece.shape[0], 128), lambda *_: (0, piece.shape[1] // 128 - 1))


def whole(shape):
    return pl.BlockSpec(shape, lambda *_: (0,) * len(shape))


def stats_body(before, first_ref, *refs):
    pieces = [first_ref] + list(refs[:-4]) if before else [first_ref] + list(refs[:-2])
    rows, local = first_ref.shape
    mean_ref, spread_ref = refs[-2], refs[-1]
    for j, p in enumerate(pieces):
        here = slice(j * rows, (j + 1) * rows)
        values = p[...].astype(F32)
        mean = jnp.sum(values, axis=1, keepdims=True) / local
        values = values - mean
        spread = jnp.sum(values * values, axis=1, keepdims=True)
        if before:
            seen = before * local
            old = refs[-4][here, :]
            gap = mean - old
            spread = refs[-3][here, :] + spread + gap * gap * (seen * local / (seen + local))
            mean = old + gap * (local / (seen + local))
        mean_ref[here, :] = mean
        spread_ref[here, :] = spread


def stats_call(pieces, seen, before, cost, name):
    rows = sum(p.shape[0] for p in pieces)
    operands = list(pieces) + list(before or ())
    return pl.pallas_call(
        lambda *refs: stats_body(seen, *refs),
        grid=(1,),
        in_specs=[features(v) for v in pieces] + [whole(v.shape) for v in before or ()],
        out_specs=[whole((rows, 1))] * 2,
        out_shape=[jax.ShapeDtypeStruct((rows, 1), F32)] * 2,
        compiler_params=pltpu.CompilerParams(vmem_limit_bytes=LIMIT << 20),
        cost_estimate=cost,
        name=name,
    )(*operands)


def stats_chain(groups, name):
    before = None
    for seen, pieces in enumerate(groups):
        before = list(stats_call(pieces, seen, before, STEP, name))
    return before


def full_norm_rows(pieces, gain_ref, hid, out_ref, first, step):
    rows, local = pieces[0].shape
    width = local * len(pieces)

    def body(i, carry):
        at = pl.multiple_of(i * step, step)
        values = [p[pl.ds(at, step), :].astype(F32) for p in pieces]
        total = values[0]
        for v in values[1:]:
            total = total + v
        mean = jnp.sum(total, axis=1, keepdims=True) / width
        centered = [v - mean for v in values]
        squares = centered[0] * centered[0]
        for c in centered[1:]:
            squares = squares + c * c
        spread = jnp.sum(squares, axis=1, keepdims=True) / width
        scale = lax.rsqrt(spread + 1e-05)
        for k, c in enumerate(centered):
            cols = pl.ds(pl.multiple_of((hid ^ k) * local, local), local)
            gain = gain_ref[:, cols].astype(F32)
            out_ref[pl.ds(first + at, step), cols] = (c * scale * gain).astype(BF16)
        return carry

    lax.fori_loop(0, rows // step, body, 0)


def norm_rows(pieces, gain_ref, mean_ref, spread_ref, hid, out_ref, first, step):
    rows, local = pieces[0].shape
    width = local * len(pieces)
    for k, p in enumerate(pieces):
        cols = pl.ds(pl.multiple_of((hid ^ k) * local, local), local)
        gain = gain_ref[:, cols].astype(F32)
        for at in range(0, rows, step):
            here = slice(first + at, first + at + step)
            scale = lax.rsqrt(spread_ref[here, :] / width + 1e-05)
            values = p[at : at + step, :].astype(F32) - mean_ref[here, :]
            out_ref[here, cols] = (values * scale * gain).astype(BF16)


def expert_body(place_ref, *refs):
    pieces = refs[:8]
    gain_ref, gate_hbm, up_hbm, down_hbm = refs[8:12]
    routed, keep_ref, send_ref = refs[12:14], refs[14], refs[15]
    normed, sums, hidden, ring, sems = refs[16:]
    rows, local = pieces[1].shape
    slots, deep = ring.shape[:2]
    width, units = gate_hbm.shape
    ups = 2 * (width // deep)
    hid, sect = place_ref[1], place_ref[2]

    def copy(n):
        if n < ups:
            src = (gate_hbm, up_hbm)[n % 2].at[n // 2 * deep : (n // 2 + 1) * deep, :]
        else:
            at = pl.multiple_of((hid ^ ORDER[n - ups]) * local, local)
            src = down_hbm.at[:, pl.ds(at, local)]
        return pltpu.make_async_copy(src, ring.at[n % slots], sems.at[n % slots])

    for n in range(slots):
        copy(n).start()
    for j in range(2):
        mine = pieces[4 * j : 4 * j + 4]
        full_norm_rows(mine, gain_ref, hid, normed, j * rows, 64)
    shares = []
    for ref in routed:
        chosen = lax.broadcasted_iota(jnp.int32, ref.shape, 1) == sect
        units_of = jnp.sum(jnp.where(chosen, ref[...].astype(F32), 0.0), axis=1, keepdims=True)
        shares.append(units_of / 256.0)
    for n in range(ups + 4):
        copy(n).wait()
        if n < ups:
            lhs = normed[:, n // 2 * deep : (n // 2 + 1) * deep]
            term = jnp.dot(lhs, ring[n % slots], preferred_element_type=F32)
            sums[n % 2] = term if n < 2 else sums[n % 2] + term
        else:
            if n == ups:
                for b in range(0, units, 128):
                    gate = sums[0, :, b : b + 128]
                    up = sums[1, :, b : b + 128]
                    hidden[:, b : b + 128] = (gate / (1.0 + jnp.exp(-gate)) * up).astype(BF16)
            out = jnp.dot(hidden[...], ring[n % slots], preferred_element_type=F32)
            keep_ref[n - ups] = out[:rows] * shares[0]
            send_ref[n - ups] = (out[rows:] * shares[1]).astype(BF16)
        if n + slots < ups + 4:
            copy(n + slots).start()


def expert_call(place, pieces, gain, gate_w, up_w, down_w, name):
    rows, local = pieces[1].shape
    width, units = gate_w.shape
    once = pl.Buffered(1)
    held = [pl.BlockSpec((rows, local), lambda *_: (0, 0), pipeline_mode=once)] * 8
    fixed = [pltpu.with_memory_space_constraint(p, pltpu.HBM) for p in pieces[:4]]
    pieces = fixed + list(pieces[4:])
    routed = [pieces[0], pieces[4]]
    shape = (4, rows, local)
    return pl.pallas_call(
        expert_body,
        grid=(1,),
        in_specs=[SMEM]
        + held
        + [whole(gain.shape)]
        + [pl.BlockSpec(memory_space=pl.ANY)] * 3
        + [routing(v) for v in routed],
        out_specs=[whole(shape)] * 2,
        out_shape=[jax.ShapeDtypeStruct(shape, F32), jax.ShapeDtypeStruct(shape, BF16)],
        scratch_shapes=[
            pltpu.VMEM((2 * rows, width), BF16),
            pltpu.VMEM((2, 2 * rows, units), F32),
            pltpu.VMEM((2 * rows, units), BF16),
            pltpu.VMEM((SLOTS, DEEP, units), BF16),
            pltpu.SemaphoreType.DMA((SLOTS,)),
        ],
        compiler_params=pltpu.CompilerParams(vmem_limit_bytes=26 << 20),
        cost_estimate=TINY,
        name=name,
    )(place, *pieces, gain, gate_w, up_w, down_w, *routed)


def sums_call(body, operands, outs, name):
    specs = []
    for i, v in enumerate(operands):
        if isinstance(v, tuple):
            operands[i], n = v
            half = (v[0].shape[0] // 2,) + v[0].shape[1:]
            specs.append(pl.BlockSpec(half, lambda *_, n=n: (n, 0, 0)))
        else:
            specs.append(whole(v.shape))
    return pl.pallas_call(
        body,
        grid=(1,),
        in_specs=specs,
        out_specs=[whole(shape) for shape, _ in outs],
        out_shape=[jax.ShapeDtypeStruct(*o) for o in outs],
        compiler_params=pltpu.CompilerParams(vmem_limit_bytes=LIMIT << 20),
        cost_estimate=TINY,
        name=name,
    )(*operands)


def core_body(keep_ref, got_ref, first_ref, second_ref):
    for n in range(4):
        out_ref = (first_ref, second_ref)[n // 2]
        out_ref[n % 2] = (keep_ref[n] + got_ref[n].astype(F32)).astype(BF16)


def chip_body(keep_ref, near_ref, far_ref, out_ref):
    for n in range(2):
        total = keep_ref[n] + near_ref[n].astype(F32) + far_ref[n].astype(F32)
        out_ref[n] = total.astype(BF16)


def pair_body(keep_ref, near_ref, far_ref, hid_ref, resid_ref, send_ref, own_ref):
    both = []
    for n in range(2):
        total = keep_ref[n + 2] + near_ref[n + 2].astype(F32) + far_ref[n].astype(F32)
        both.append(total + hid_ref[n].astype(F32))
    send_ref[...] = both[0].astype(BF16)
    own_ref[...] = resid_ref[...].astype(F32) + both[1]


def last_body(own_ref, got_ref, out_ref):
    out_ref[...] = (own_ref[...] + got_ref[...].astype(F32)).astype(BF16)


def stage_body(*refs):
    count = (len(refs) - 2) // 2
    copies = [
        pltpu.make_async_copy(refs[i], refs[count + i], refs[-1].at[i]) for i in range(count)
    ]
    for c in copies:
        c.start()
    refs[-2][...] = jnp.zeros_like(refs[-2])
    for c in copies:
        c.wait()


def stage_call(arrays, name):
    return pl.pallas_call(
        stage_body,
        in_specs=[pl.BlockSpec(memory_space=pl.ANY)] * len(arrays),
        out_specs=[VMEM] * (len(arrays) + 1),
        out_shape=[pltpu.VMEM(a.shape, a.dtype) for a in arrays]
        + [jax.ShapeDtypeStruct((8, 128), F32)],
        scratch_shapes=[pltpu.SemaphoreType.DMA((len(arrays),))],
        compiler_params=pltpu.CompilerParams(vmem_limit_bytes=LIMIT << 20),
        cost_estimate=TINY,
        name=name,
    )(*arrays)


def attend_body(place_ref, *refs):
    pieces = refs[:4]
    mean_ref, spread_ref, gain_ref, cos_ref, sin_ref, bias_ref = refs[4:10]
    weights = list(refs[10:23])
    last_hbm, out_ref, normed, total, last_ref, sem = refs[24:30]
    weights.append(last_ref)
    rows, local = pieces[0].shape
    half = local // 2
    group, hid, sect = place_ref[0], place_ref[1], place_ref[2]
    copy = pltpu.make_async_copy(last_hbm, last_ref, sem.at[0])
    copy.start()
    norm_rows(pieces, gain_ref, mean_ref, spread_ref, hid, normed, 0, 64)

    def rows_of(at, count):
        return normed[:, pl.ds(pl.multiple_of(at, 512), count)]

    starts = [(sect ^ j) * local for j in range(4)]
    mine, other = group * half, (1 - group) * half
    halves = [rows_of(starts[j] + o, half) for j in (2, 3) for o in (mine, other)]
    wholes = [rows_of(at, local) for at in starts]
    plan = []
    for c in range(2):
        cols = slice(c * half, (c + 1) * half)
        plan.append([(wholes[i], i, cols) for i in range(2)])
        plan[c] += [(halves[i], 2 + 4 * c + i, slice(0, half)) for i in range(4)]
    plan.append([(wholes[i], 10 + i, slice(0, half)) for i in range(4)])
    for c, terms in enumerate(plan):
        acc = None
        for lhs, n, cols in terms:
            if n == 13:
                copy.wait()
            term = jnp.dot(lhs, weights[n][:, cols], preferred_element_type=F32)
            acc = term if acc is None else acc + term
        total[:, c * half : (c + 1) * half] = acc
    heads = local // HD
    kv_heads = (total.shape[1] - local) // (2 * HD)
    cos, sin, bias = cos_ref[...], sin_ref[...], bias_ref[...]

    def turned(at):
        x = total[:, at : at + HD]
        return (x * cos + pltpu.roll(x, HD // 2, 1) * sin).astype(BF16)

    for g in range(kv_heads):
        key = turned(local + g * HD)
        at = local + (kv_heads + g) * HD
        val = total[:, at : at + HD].astype(BF16)
        for r in range(heads // kv_heads):
            at = (g * (heads // kv_heads) + r) * HD
            scores = lax.dot_general(
                turned(at), key, (((1,), (1,)), ((), ())), preferred_element_type=F32
            ) * (1.0 / math.sqrt(HD)) + bias
            weight = jnp.exp(scores - jnp.max(scores, axis=1, keepdims=True))
            probs = (weight / jnp.sum(weight, axis=1, keepdims=True)).astype(BF16)
            mixed = jnp.dot(probs, val, preferred_element_type=F32)
            out_ref[:, at : at + HD] = mixed.astype(BF16)


def attend_call(place, pieces, stats, gain, cos, sin, bias, weights):
    rows, local = pieces[0].shape
    return pl.pallas_call(
        attend_body,
        grid=(1,),
        in_specs=[SMEM]
        + [whole(v.shape) for v in (*pieces, *stats, gain, cos, sin, bias)]
        + [VMEM] * (len(weights) - 2)
        + [whole((8, 128)), pl.BlockSpec(memory_space=pl.ANY)],
        out_specs=whole((rows, local)),
        out_shape=jax.ShapeDtypeStruct((rows, local), BF16),
        scratch_shapes=[pltpu.VMEM((rows, 4 * local), BF16), pltpu.VMEM((rows, 3 * local // 2), F32)]
        + [pltpu.VMEM(weights[-1].shape, BF16)]
        + [pltpu.SemaphoreType.DMA((1,))],
        compiler_params=pltpu.CompilerParams(vmem_limit_bytes=20 << 20),
        cost_estimate=TINY,
        name="attend",
    )(place, *pieces, *stats, gain, cos, sin, bias, *weights)


def swap(value, axis, size, by):
    return lax.ppermute(value, axis, [(i, i ^ by) for i in range(size)])


def tie(*values):
    return lax.optimization_barrier(values)


def position_tables(lengths, count):
    ends = jnp.cumsum(lengths, dtype=jnp.int32)
    places = jnp.arange(count, dtype=jnp.int32)
    past = (places[:, None] >= ends[None, :]).astype(jnp.int32)
    doc_ids = jnp.sum(past, axis=1, dtype=jnp.int32)
    starts = jnp.sum(past * lengths[None, :], axis=1, dtype=jnp.int32)
    position = (places - starts).astype(F32)
    half = HD // 2
    freqs = jnp.exp(jnp.arange(half, dtype=F32) * (-2.0 * math.log(10000.0) / HD))
    angles = position[:, None] * freqs[None, :]
    cosine = jnp.cos(angles)
    sine = jnp.sin(angles)
    allowed = (doc_ids[:, None] == doc_ids[None, :]) & (places[None, :] <= places[:, None])
    bias = jnp.where(allowed, 0.0, -jnp.inf).astype(F32)
    return (
        jnp.concatenate([cosine, cosine], axis=1),
        jnp.concatenate([-sine, sine], axis=1),
        bias,
    )


def on_grid(
    resid, moe_gain, routes, gate_q, doc_lengths, w_gate, w_up, w_down, attn_gain, w_q, w_k, w_v
):
    tokens, local = resid.shape
    half = local // 2
    group = lax.axis_index("groups")
    sect = lax.axis_index("sect")
    hid = lax.axis_index("hid")
    place = jnp.stack([group, hid, sect]).astype(jnp.int32)

    over_hid = lambda v, by: swap(v, "hid", 4, by)
    over_core = lambda v: swap(v, "sect", 4, 1)
    over_chip = lambda v: swap(v, "sect", 4, 2)
    over_group = lambda v: swap(v, "groups", 2, 1)

    def half_of(w, c):
        return lax.dynamic_slice(w, (group * half, c * half), (half, half))

    here, there, here_core, there_core = ([None] * 2 for _ in range(4))
    gate_w, up_w, down_w = (
        pltpu.with_memory_space_constraint(w[0], pltpu.HBM) for w in (w_gate, w_up, w_down)
    )

    first, second = over_hid(resid, 1), over_hid(resid, 2)
    experts = jnp.arange(128, dtype=jnp.int32)
    units = jnp.sum(jnp.where(routes[:, :, None] == experts, gate_q[:, :, None], 0), axis=1)
    marked = jnp.concatenate([resid, units.astype(BF16)], axis=1)
    far_own = over_chip(marked)
    here[0] = over_chip(half_of(w_q, 0))
    w_kv = jnp.concatenate([w_k, w_v], axis=1)
    waiting = [half_of(w_q, 1)]
    tables = position_tables(doc_lengths[0], tokens)
    first, second, far_own, marked, w_q, w_kv, *held = tie(
        first, second, far_own, marked, w_q, w_kv, *waiting, *tables
    )
    waiting, tables = held[:1], held[1:]
    third = over_hid(second, 1)
    far = [far_own, over_chip(first), over_chip(second), None]
    near_pair = [over_core(marked), over_core(first), over_core(second), None]
    third, far[1], here[0] = tie(third, far[1], here[0])
    far[3], near_pair[3] = over_chip(third), over_core(third)
    near = [marked, first, second, third]
    far_pair = [over_core(far[0]), over_core(far[1]), None, None]

    gain = moe_gain.reshape(1, -1)
    weights = (gate_w, up_w, down_w)
    near_keep, near_send = expert_call(place, near + near_pair, gain, *weights, "near")
    near_send, far_pair[0], far_pair[1], *far = tie(near_send, far_pair[0], far_pair[1], *far)
    far_pair[2:] = [over_core(v) for v in far[2:]]
    far[3], waiting[0] = tie(far[3], waiting[0])
    here[1] = over_chip(waiting[0])
    far_keep, far_send = expert_call(place, far + far_pair, gain, *weights, "far")
    far_send, near_send, here[0], here[1] = tie(far_send, near_send, here[0], here[1])

    rows_of = (2, tokens, local)
    near_got, there[0] = over_core(near_send), over_group(here[0])
    operands = [far_keep, over_core(far_send)]
    summed = list(sums_call(core_body, operands, [(rows_of, BF16)] * 2, "sum_core"))
    got = over_chip(summed[0])
    got, near_got, there[0], here[0], here[1], summed[1] = tie(
        got, near_got, there[0], here[0], here[1], summed[1]
    )
    got_rest, there[1] = over_chip(summed[1]), over_group(here[1])
    here_core[0], there_core[0] = over_core(here[0]), over_core(there[0])
    operands = [near_keep, near_got, got]
    (part,) = sums_call(chip_body, operands, [(rows_of, BF16)], "sum_chip")
    part = over_hid(part, 1)
    part, got_rest, there[1], here_core[0], there_core[0], here[1], w_q, w_kv = tie(
        part, got_rest, there[1], here_core[0], there_core[0], here[1], w_q, w_kv
    )
    kv_far, q_near = over_chip(w_kv), over_core(w_q)
    here_core[1], there_core[1] = over_core(here[1]), over_core(there[1])
    operands = [near_keep, near_got, got_rest, part, resid]
    one = (tokens, local)
    send, own = sums_call(pair_body, operands, [(one, BF16), (one, F32)], "sum_pair")
    send = over_hid(send, 2)
    send, q_near, here_core[1], there_core[1], w_kv = tie(
        send, q_near, here_core[1], there_core[1], w_kv
    )
    (new_local,) = sums_call(last_body, [own, send], [(one, BF16)], "sum_hid")

    kv_near = over_core(w_kv)
    second = over_hid(new_local, 2)
    rows = [new_local, over_hid(new_local, 1), second, None]
    rows[2], rows[1], kv_near, kv_far = tie(rows[2], rows[1], kv_near, kv_far)
    rows[3] = over_hid(rows[2], 1)
    moved = [(here[c], there[c], here_core[c], there_core[c]) for c in range(2)]
    proj = [w_q, q_near, *moved[0], *moved[1], w_kv, kv_near, kv_far]
    *proj, token = stage_call(proj, "stage")
    rows[3], token = tie(rows[3], token)
    proj += [token, over_core(kv_far)]
    stats = stats_chain([[r] for r in rows], "stats_next")
    gain = attn_gain.reshape(1, -1)
    context = attend_call(place, rows, stats, gain, *tables, proj)
    return (new_local, context)


def layer_norm(values, gain):
    center = values - jnp.mean(values, axis=1, keepdims=True)
    spread = jnp.mean(center * center, axis=1, keepdims=True)
    return (center * lax.rsqrt(spread + 1e-05) * gain.astype(jnp.float32)).astype(jnp.bfloat16)


def slot_targets(route_rows, experts, capacity):
    flat = route_rows.reshape(-1)
    onehot = (flat[:, None] == jnp.arange(experts, dtype=jnp.int32)[None, :]).astype(jnp.int32)
    before = jnp.cumsum(onehot, axis=0, dtype=jnp.int32) - onehot
    return flat * capacity + jnp.sum(before * onehot, axis=1, dtype=jnp.int32)


def source_rows(targets, experts, capacity):
    count = targets.shape[0]
    filler = jnp.full((experts * capacity,), count, jnp.int32)
    return filler.at[targets].set(jnp.arange(count, dtype=jnp.int32)) // 2


def rotate(values, position, head):
    count = values.shape[0]
    split_heads = values.reshape(count, -1, head)
    half = head // 2
    freqs = jnp.exp(jnp.arange(half, dtype=jnp.float32) * (-2.0 * math.log(10000.0) / head))
    angles = position[:, None, None] * freqs[None, None, :]
    cosine = jnp.cos(angles)
    sine = jnp.sin(angles)
    first = split_heads[:, :, :half]
    second = split_heads[:, :, half:]
    turned = jnp.concatenate(
        [first * cosine - second * sine, second * cosine + first * sine], axis=2
    )
    return turned.reshape(count, -1)


def attend(query, keys, vals, lengths, head, group):
    count = query.shape[0]
    kv_heads = keys.shape[1] // head
    ends = jnp.cumsum(lengths, dtype=jnp.int32)
    places = jnp.arange(count, dtype=jnp.int32)
    after = (places[:, None] >= ends[None, :]).astype(jnp.int32)
    doc_ids = jnp.sum(after, axis=1, dtype=jnp.int32)
    starts = jnp.sum(after * lengths[None, :], axis=1, dtype=jnp.int32)
    position = (places - starts).astype(jnp.float32)
    rotated_q = (
        rotate(query, position, head).astype(jnp.bfloat16).reshape(count, kv_heads, group, head)
    )
    rotated_k = rotate(keys, position, head).astype(jnp.bfloat16).reshape(count, kv_heads, head)
    value_heads = vals.reshape(count, kv_heads, head)
    allowed = (doc_ids[:, None] == doc_ids[None, :]) & (places[None, :] <= places[:, None])
    scores = jnp.einsum(
        "tkgd,skd->kgts", rotated_q, rotated_k, preferred_element_type=jnp.float32
    ) * (1.0 / math.sqrt(head))
    scores = jnp.where(allowed[None, None], scores, -jnp.inf)
    highest = jnp.max(scores, axis=3, keepdims=True)
    weights = jnp.exp(scores - highest)
    probs = (weights / jnp.sum(weights, axis=3, keepdims=True)).astype(jnp.bfloat16)
    mixed = jnp.einsum("kgts,skd->tkgd", probs, value_heads, preferred_element_type=jnp.float32)
    return mixed.astype(jnp.bfloat16).reshape(count, -1)


def on_device(
    resid, moe_gain, routes, gate_q, doc_lengths, w_gate, w_up, w_down, attn_gain, w_q, w_k, w_v
):
    sections = lax.axis_size("sect")
    slices = lax.axis_size("hid")
    tokens_here, local_width = resid.shape
    width = local_width * slices
    capacity = 4 * tokens_here // sections
    entry = lax.all_gather(resid, "hid", axis=1, tiled=True)
    normed = layer_norm(entry.astype(jnp.float32), moe_gain)
    targets = slot_targets(routes, sections, capacity)
    sources = source_rows(targets, sections, capacity)
    padded = jnp.concatenate([normed, jnp.zeros((1, width), jnp.bfloat16)], axis=0)
    gate_w = w_gate[0]
    up_w = w_up[0]
    down_w = w_down[0]
    outgoing = padded[sources].reshape(sections, capacity, width)
    arrived = lax.all_to_all(outgoing, "sect", split_axis=0, concat_axis=0, tiled=True).reshape(
        sections * capacity, width
    )
    gate = jnp.dot(arrived, gate_w, preferred_element_type=jnp.float32)
    up = jnp.dot(arrived, up_w, preferred_element_type=jnp.float32)
    hidden = (jax.nn.silu(gate) * up).astype(jnp.bfloat16)
    weights = gate_q.reshape(-1).astype(jnp.float32) / 256.0
    own_resid = resid.astype(jnp.float32)
    outputs = jnp.dot(hidden, down_w, preferred_element_type=jnp.float32)
    mine = lax.psum_scatter(outputs, "hid", scatter_dimension=1, tiled=True)
    returned = lax.all_to_all(
        mine.reshape(sections, capacity, local_width),
        "sect",
        split_axis=0,
        concat_axis=0,
        tiled=True,
    )
    picked = returned.reshape(sections * capacity, local_width)[targets]
    mixture = jnp.sum((picked * weights[:, None]).reshape(tokens_here, 2, local_width), axis=1)
    new_local = (own_resid + mixture).astype(jnp.bfloat16)
    full_rows = lax.all_gather(new_local, "hid", axis=1, tiled=True)
    normed_next = layer_norm(full_rows.astype(jnp.float32), attn_gain)
    query = jnp.dot(
        normed_next,
        lax.all_gather(w_q, "sect", axis=0, tiled=True),
        preferred_element_type=jnp.float32,
    )
    keys = jnp.dot(
        normed_next,
        lax.all_gather(w_k, "sect", axis=0, tiled=True),
        preferred_element_type=jnp.float32,
    )
    vals = jnp.dot(
        normed_next,
        lax.all_gather(w_v, "sect", axis=0, tiled=True),
        preferred_element_type=jnp.float32,
    )
    context = attend(query, keys, vals.astype(jnp.bfloat16), doc_lengths[0], HD, H // KVH)
    return (new_local, context)


def solution(mesh):
    in_specs = (
        P(("groups", "sect"), "hid"),
        P(),
        P(("groups", "sect"), None),
        P(("groups", "sect"), None),
        P(("groups", "sect"), None),
        P("sect", None, "hid"),
        P("sect", None, "hid"),
        P("sect", "hid", None),
        P(),
        P("sect", "hid"),
        P("sect", "hid"),
        P("sect", "hid"),
    )
    out_specs = (P(("groups", "sect"), "hid"), P(("groups", "sect"), "hid"))
    plan = on_device
    if dict(mesh.shape) == {"groups": 2, "sect": 4, "hid": 4}:
        plan = on_grid
    return jax.shard_map(
        plan, mesh=mesh, in_specs=in_specs, out_specs=out_specs, check_vma=False
    )
```
